512 devices in a mesh: ta: 8 (over z_hi, x), ha: 64 (over y, z_lo, core).
Axes of the slice: x: 4, y: 4, z: 16 (z_hi: 2, z_lo: 8; z = z_hi * 8 + z_lo), core: 2. Of those that a mesh axis runs over, the one named last changes fastest.
Arguments:
- query: bfloat16 [64, 64, 16, 2560], P('ta', 'ha'), may hold values from -2.5 to 2.5
- key_value: bfloat16 [64, 64, 16, 5120], P('ta', 'ha'), may hold values from -2.5 to 2.5
- out_grad: bfloat16 [64, 64, 16, 2560], P('ta', 'ha'), may hold values from -96 to 96
- text_kv: bfloat16 [32, 5120], replicated, may hold values from -2.5 to 2.5
- tile_reach: int32 [64, 64, 2], replicated, may hold values from 0 to 1
- text_len: int32 [64, 64], replicated, may hold values from 1 to 32
Outputs:
- query_grad: bfloat16 [64, 64, 16, 2560], P('ta', 'ha')
- key_value_grad: bfloat16 [64, 64, 16, 5120], P('ta', 'ha')
- text_grad: bfloat16 [32, 5120], P(None, ('ta', 'ha'))
The draws below stay inside these ranges and needn't reach their ends.
Inputs may be any that keep to these rules, and one draw needn't show every extreme that they name: tile_reach[f, r, 0] and tile_reach[f, r, 1] are the frames and rows that the window of the tile at (f, r) reaches to each side. The tile at (f, r) sees the first text_len[f, r] text tokens.
All inputs are finite; a program needn't handle non-finite values.
Results may differ from the reference program's by a relative error of at most 0.008.
Values may be sent and summed in bfloat16 or wider, within the bound.
A program may use at most 128 MiB of HBM per device.

```python
import math
import jax
import jax.numpy as jnp
from jax import lax

HEADS = 20
HD = 128
COLS = 16
TEXT = 32
FRAMES = 64
HROWS = 64


def place_ends(values, key, smallest, high):
    place = [jax.random.randint(jax.random.fold_in(key, axis), (), 0, length) for axis, length in enumerate(values.shape)]
    main_axis = values.shape.index(max(values.shape))
    next_to = place[:main_axis] + [(place[main_axis] + 1) % values.shape[main_axis]] + place[main_axis + 1:]
    return values.at[tuple(place)].set(smallest).at[tuple(next_to)].set(high)


def block_scale(key, shape, split, smallest, high):
    gain, own = 1.0, jax.random.fold_in(key, 6)
    for position, parts in split:
        draws = jnp.exp(jax.random.uniform(jax.random.fold_in(own, position), (parts,), jnp.float32, smallest / len(split), high / len(split)))
        gain = gain * jnp.repeat(draws, shape[position] // parts).reshape([-1 if axis == position else 1 for axis in range(len(shape))])
    return gain


def noise(key, extent, deviation, most, cuts=(), kind=jnp.bfloat16):
    loudness = block_scale(key, extent, cuts, -0.22, 0.18) if cuts else 1.0
    values = jax.random.normal(key, extent, jnp.float32) * deviation * loudness
    return jnp.minimum(jnp.maximum(values, -most), most).astype(kind)


def setup_inputs(seed: int = 0) -> dict:
    streams_of = jax.random.split(jax.random.key(seed), 7)
    return {
        "query": noise(streams_of[0], (FRAMES, HROWS, COLS, HEADS * HD), 1.0, 2.5, ((0, 8), (1, 64))),
        "key_value": noise(streams_of[1], (FRAMES, HROWS, COLS, 2 * HEADS * HD), 1.0, 2.5, ((0, 8), (1, 64))),
        "out_grad": noise(streams_of[2], (FRAMES, HROWS, COLS, HEADS * HD), 16.0, 96.0, ((0, 8), (1, 64))),
        "text_kv": noise(streams_of[3], (TEXT, 2 * HEADS * HD), 1.0, 2.5),
        "tile_reach": place_ends(jax.random.randint(streams_of[4], (FRAMES, HROWS, 2), 0, 2), jax.random.fold_in(streams_of[4], 1), 0, 1).astype(jnp.int32),
        "text_len": place_ends(jax.random.randint(streams_of[5], (FRAMES, HROWS), 1, TEXT + 1), jax.random.fold_in(streams_of[5], 1), 1, TEXT).astype(jnp.int32),
    }


frame_steps = (0, 0, 0, 1, 1, 1, 2, 2, 2)
row_steps = (0, 1, 2, 0, 1, 2, 0, 1, 2)

def window_stack(padded, anchor, row_count):
    slab = lax.dynamic_slice_in_dim(padded, anchor, 3, 0)
    return jnp.stack([slab[lead_step, row_step:row_step + row_count] for lead_step, row_step in zip(frame_steps, row_steps)], axis=1)

def round_half(values):
    halved = values.astype(jnp.bfloat16)
    return lax.optimization_barrier(halved).astype(jnp.float32)

def reference(query, key_value, out_grad, text_kv, tile_reach, text_len):
    feature_width = HEADS * HD
    score_scale = 1.0 / math.sqrt(HD)
    row_count = HROWS
    frame_shift = jnp.array(frame_steps, dtype=jnp.int32) - 1
    row_shift = jnp.array(row_steps, dtype=jnp.int32) - 1
    row_ids = jnp.arange(row_count, dtype=jnp.int32)
    text_keys = text_kv[:, :feature_width].reshape(TEXT, HEADS, HD).astype(jnp.float32)
    text_values = text_kv[:, feature_width:].reshape(TEXT, HEADS, HD).astype(jnp.float32)
    spacing = ((1, 1), (1, 1), (0, 0), (0, 0))
    kv_padded = jnp.pad(key_value, spacing)

    def query_side(frame_id):
        queries = lax.dynamic_index_in_dim(query, frame_id, 0, keepdims=False).reshape(row_count, COLS, HEADS, HD).astype(jnp.float32)
        grads = lax.dynamic_index_in_dim(out_grad, frame_id, 0, keepdims=False).reshape(row_count, COLS, HEADS, HD).astype(jnp.float32)
        window = window_stack(kv_padded, frame_id, row_count)
        key_rows = window[..., :feature_width].reshape(row_count, 9 * COLS, HEADS, HD).astype(jnp.float32)
        values = window[..., feature_width:].reshape(row_count, 9 * COLS, HEADS, HD).astype(jnp.float32)
        reach_here = lax.dynamic_index_in_dim(tile_reach, frame_id, 0, keepdims=False)
        key_frames = frame_id + frame_shift
        key_row = row_ids[:, None] + row_shift[None, :]
        visible = ((key_frames >= 0) & (key_frames < FRAMES))[None, :] & (key_row >= 0) & (key_row < HROWS)
        visible = visible & (jnp.abs(frame_shift)[None, :] <= reach_here[:, 0:1]) & (jnp.abs(row_shift)[None, :] <= reach_here[:, 1:2])
        visible = jnp.repeat(visible, COLS, axis=1)[:, None, None, :]
        length = lax.dynamic_index_in_dim(text_len, frame_id, 0, keepdims=False)
        text_visible = (jnp.arange(TEXT, dtype=jnp.int32)[None, :] < length[:, None])[:, None, None, :]
        scores = jnp.einsum('rchd,rkhd->rhck', queries, key_rows) * score_scale
        text_scores = jnp.einsum('rchd,thd->rhct', queries, text_keys) * score_scale
        exp_total = lax.optimization_barrier(jnp.sum(jnp.where(visible, jnp.exp(scores), 0.0), axis=-1)) + lax.optimization_barrier(jnp.sum(jnp.where(text_visible, jnp.exp(text_scores), 0.0), axis=-1))
        log_total = jnp.log(exp_total)
        weights = jnp.where(visible, jnp.exp(scores - log_total[..., None]), 0.0)
        text_weights = jnp.where(text_visible, jnp.exp(text_scores - log_total[..., None]), 0.0)
        weights_half = round_half(weights)
        text_half = round_half(text_weights)
        attended = jnp.einsum('rhck,rkhd->rchd', weights_half, values) + jnp.einsum('rhct,thd->rchd', text_half, text_values)
        row_delta = jnp.transpose(lax.optimization_barrier(jnp.sum(grads * attended, axis=-1)), (0, 2, 1))
        dprob = jnp.einsum('rchd,rkhd->rhck', grads, values)
        text_dprob = jnp.einsum('rchd,thd->rhct', grads, text_values)
        dscore = round_half(weights * (dprob - row_delta[..., None]))
        text_dscore = round_half(text_weights * (text_dprob - row_delta[..., None]))
        query_sum = jnp.einsum('rhck,rkhd->rchd', dscore, key_rows) + jnp.einsum('rhct,thd->rchd', text_dscore, text_keys)
        query_part = (score_scale * query_sum).reshape(row_count, COLS, feature_width).astype(jnp.bfloat16)
        text_key_grad = score_scale * jnp.einsum('rhct,rchd->thd', text_dscore, queries)
        text_value_grad = jnp.einsum('rhct,rchd->thd', text_half, grads)
        text_part = jnp.concatenate([text_key_grad.reshape(TEXT, feature_width), text_value_grad.reshape(TEXT, feature_width)], axis=1)
        return (query_part, log_total, row_delta, text_part)
    frame_ids = jnp.arange(FRAMES, dtype=jnp.int32)
    query_grad, log_totals, deltas, text_parts = lax.map(query_side, frame_ids)
    query_padded = jnp.pad(query, spacing)
    grad_padded = jnp.pad(out_grad, spacing)
    log_padded = jnp.pad(log_totals, spacing)
    delta_padded = jnp.pad(deltas, spacing)
    reach_padded = jnp.pad(tile_reach, ((1, 1), (1, 1), (0, 0)))

    def key_side(frame_id):
        kv_here = lax.dynamic_index_in_dim(key_value, frame_id, 0, keepdims=False)
        key_rows = kv_here[..., :feature_width].reshape(row_count, COLS, HEADS, HD).astype(jnp.float32)
        values = kv_here[..., feature_width:].reshape(row_count, COLS, HEADS, HD).astype(jnp.float32)
        queries = window_stack(query_padded, frame_id, row_count).reshape(row_count, 9 * COLS, HEADS, HD).astype(jnp.float32)
        grads = window_stack(grad_padded, frame_id, row_count).reshape(row_count, 9 * COLS, HEADS, HD).astype(jnp.float32)
        log_here = jnp.transpose(window_stack(log_padded, frame_id, row_count), (0, 2, 1, 3)).reshape(row_count, HEADS, 9 * COLS)
        delta_here = jnp.transpose(window_stack(delta_padded, frame_id, row_count), (0, 2, 1, 3)).reshape(row_count, HEADS, 9 * COLS)
        reach_here = window_stack(reach_padded, frame_id, row_count)
        query_frames = frame_id + frame_shift
        query_row = row_ids[:, None] + row_shift[None, :]
        visible = ((query_frames >= 0) & (query_frames < FRAMES))[None, :] & (query_row >= 0) & (query_row < HROWS)
        visible = visible & (jnp.abs(frame_shift)[None, :] <= reach_here[..., 0]) & (jnp.abs(row_shift)[None, :] <= reach_here[..., 1])
        visible = jnp.repeat(visible, COLS, axis=1)[:, None, :, None]
        scores = jnp.einsum('rqhd,rchd->rhqc', queries, key_rows) * score_scale
        weights = jnp.where(visible, jnp.exp(scores - log_here[..., None]), 0.0)
        weights_half = round_half(weights)
        dprob = jnp.einsum('rqhd,rchd->rhqc', grads, values)
        dscore = round_half(weights * (dprob - delta_here[..., None]))
        key_grad = score_scale * jnp.einsum('rhqc,rqhd->rchd', dscore, queries)
        value_grad = jnp.einsum('rhqc,rqhd->rchd', weights_half, grads)
        return jnp.concatenate([key_grad.reshape(row_count, COLS, feature_width), value_grad.reshape(row_count, COLS, feature_width)], axis=-1).astype(jnp.bfloat16)
    key_value_grad = lax.map(key_side, frame_ids)
    text_grad = lax.optimization_barrier(jnp.sum(text_parts, axis=0)).astype(jnp.bfloat16)
    return (query_grad, key_value_grad, text_grad)
```

```python
import functools
import math

import jax
import jax.numpy as jnp
from jax import lax
from jax.experimental import pallas as pl
from jax.experimental.pallas import tpu as pltpu
from jax.sharding import PartitionSpec as P

HD = 128
MESH = pl.DeviceIdType.MESH
F32 = jnp.float32
BF16 = jnp.bfloat16

HEADS_PER_GROUP = 2
AHEAD = 2
LAG_TOTALS = 1
LAG_GRADS = 2
LAG_FOLD = 4


def both_last(a, b):
    return lax.dot_general(a, b, (((1,), (1,)), ((), ())), preferred_element_type=F32)


def both_first(a, b):
    return lax.dot_general(a, b, (((0,), (0,)), ((), ())), preferred_element_type=F32)


def plain(a, b):
    return lax.dot_general(a, b, (((1,), (0,)), ((), ())), preferred_element_type=F32)


def attention_kernel(
    nt,
    nh,
    q_hbm,
    kv_hbm,
    do_hbm,
    text,
    lanes,
    dq_out,
    dkv_out,
    text_out,
    q_all,
    do_all,
    kv_all,
    bias,
    e_all,
    dp_all,
    stat_send,
    stat_recv,
    stat_own,
    coef_recv,
    coef_own,
    dq_send,
    dq_recv,
    dq_own,
    dkv_send,
    dkv_recv,
    dkv_own,
    own_sem,
    row_s,
    row_r,
    fr_s,
    fr_r,
    stat_s,
    stat_r,
    coef_s,
    coef_r,
    dq_s,
    dq_r,
    dkv_s,
    dkv_r,
):
    frames, columns = q_all.shape[1], q_all.shape[2]
    width = q_all.shape[3]
    tokens = frames * columns
    texts = text.shape[0]
    heads = width // HD
    hg = HEADS_PER_GROUP
    groups = heads // hg
    gw = hg * HD
    scale = 1.0 / math.sqrt(HD)
    keys = texts + (frames + 2) * columns
    ta, ha = lax.axis_index("ta"), lax.axis_index("ha")
    has_dn, has_up = ha > 0, ha < nh - 1
    has_prev, has_next = ta > 0, ta < nt - 1
    dn, up = {"ha": ha - 1}, {"ha": ha + 1}
    prev, nxt = {"ta": ta - 1}, {"ta": ta + 1}

    own_copies = [
        pltpu.make_async_copy(q_hbm.at[:, 0], q_all.at[1], own_sem.at[0]),
        pltpu.make_async_copy(do_hbm.at[:, 0], do_all.at[1], own_sem.at[1]),
        pltpu.make_async_copy(kv_hbm.at[:, 0], kv_all.at[pl.ds(1, frames)], own_sem.at[2]),
    ]
    for copy in own_copies:
        copy.start()

    barrier = pltpu.get_barrier_semaphore()
    sides = ((has_dn, dn), (has_up, up), (has_prev, prev), (has_next, nxt))
    for has, where in sides:

        @pl.when(has)
        def _(where=where):
            pl.semaphore_signal(barrier, inc=1, device_id=where, device_id_type=MESH)

    pl.semaphore_wait(barrier, sum(has.astype(jnp.int32) for has, _ in sides))

    def at(g, base=0):
        return pl.ds(pl.multiple_of(base + g * gw, HD), gw)

    def remote(src, dst, send, recv, where):
        return pltpu.make_async_remote_copy(
            src_ref=src,
            dst_ref=dst,
            send_sem=send,
            recv_sem=recv,
            device_id=where,
            device_id_type=MESH,
        )

    def row_copies(g, side, where):
        slot = 0 if side == 0 else 2
        return [
            remote(q_hbm.at[:, 0, :, at(g)], q_all.at[slot, :, :, at(g)], row_s.at[side, 0, g], row_r.at[side, 0, g], where),
            remote(do_hbm.at[:, 0, :, at(g)], do_all.at[slot, :, :, at(g)], row_s.at[side, 1, g], row_r.at[side, 1, g], where),
        ]

    def frame_copies(g, side, where):
        source = frames - 1 if side == 0 else 0
        slot = 0 if side == 0 else frames + 1
        return [
            remote(
                kv_hbm.at[source, 0, :, at(g, base)],
                kv_all.at[slot, :, at(g, base)],
                fr_s.at[side, i, g],
                fr_r.at[side, i, g],
                where,
            )
            for i, base in enumerate((0, width))
        ]

    def stat_copy(g, side, where):
        return remote(stat_send.at[side, g], stat_recv.at[side, g], stat_s.at[side, g], stat_r.at[side, g], where)

    def coef_copy(g, side, where):
        return remote(coef_own.at[g], coef_recv.at[side, g], coef_s.at[side, g], coef_r.at[side, g], where)

    def dq_copy(g, side, where):
        return remote(
            dq_send.at[side, :, :, at(g)], dq_recv.at[side, :, :, at(g)], dq_s.at[side, g], dq_r.at[side, g], where
        )

    def dkv_copies(g, side, where):
        return [
            remote(
                dkv_send.at[side, :, at(g, base)],
                dkv_recv.at[side, :, at(g, base)],
                dkv_s.at[side, i, g],
                dkv_r.at[side, i, g],
                where,
            )
            for i, base in enumerate((0, width))
        ]

    row_routes = ((0, has_up, up, has_dn), (1, has_dn, dn, has_up))
    frame_routes = ((0, has_next, nxt, has_prev), (1, has_prev, prev, has_next))

    def as_list(x):
        return x if isinstance(x, list) else [x]

    def start(make, routes, g):
        for side, has, where, _ in routes:

            @pl.when(has)
            def _(side=side, where=where):
                for copy in as_list(make(g, side, where)):
                    copy.start()

    def arrived(make, routes, g):
        for side, _, where, has in routes:

            @pl.when(has)
            def _(side=side, where=where):
                for copy in as_list(make(g, side, where)):
                    copy.wait_recv()

    def sent(make, routes, g):
        for side, has, where, _ in routes:

            @pl.when(has)
            def _(side=side, where=where):
                for copy in as_list(make(g, side, where)):
                    copy.wait_send()

    def forward(g):
        start(frame_copies, frame_routes, g)
        start(row_copies, row_routes, g)

    for g in range(min(AHEAD, groups)):
        forward(g)

    for side, _, _, has in row_routes:

        @pl.when(jnp.logical_not(has))
        def _(side=side):
            slot = 0 if side == 0 else 2
            q_all[slot] = jnp.zeros(q_all.shape[1:], BF16)
            do_all[slot] = jnp.zeros(do_all.shape[1:], BF16)
            stat_recv[side] = jnp.zeros(stat_recv.shape[1:], F32)
            coef_recv[side] = jnp.zeros(coef_recv.shape[1:], F32)
            dq_recv[side] = jnp.zeros(dq_recv.shape[1:], BF16)

    for side, _, _, has in frame_routes:

        @pl.when(jnp.logical_not(has))
        def _(side=side):
            slot = 0 if side == 0 else frames + 1
            kv_all[slot] = jnp.zeros(kv_all.shape[1:], BF16)
            dkv_recv[side] = jnp.zeros(dkv_recv.shape[1:], BF16)

    line = lax.broadcasted_iota(jnp.int32, (keys, 3 * tokens), 0)
    lane = lax.broadcasted_iota(jnp.int32, (keys, 3 * tokens), 1)
    query_frame = lax.rem(lane, tokens) // columns
    key_frame = (line - texts + columns) // columns - 2
    gap = jnp.abs(key_frame - query_frame)
    inside = ((key_frame >= 0) | has_prev) & ((key_frame < frames) | has_next)
    latent_seen = (line >= texts) & inside & (gap <= lanes[0:1, :])
    text_seen = (line < texts) & (line < lanes[1:2, :])
    bias[...] = jnp.where(latent_seen | text_seen, 0.0, -1e30)
    for copy in own_copies:
        copy.wait()

    def operands(h):
        cols = pl.ds(pl.multiple_of(h * HD, HD), HD)
        vcols = pl.ds(pl.multiple_of(width + h * HD, HD), HD)
        q3 = q_all[:, :, :, cols].reshape(3 * tokens, HD)
        do3 = do_all[:, :, :, cols].reshape(3 * tokens, HD)
        kall = jnp.concatenate([text[:, cols], kv_all[:, :, cols].reshape(-1, HD)], axis=0)
        vall = jnp.concatenate([text[:, vcols], kv_all[:, :, vcols].reshape(-1, HD)], axis=0)
        return q3, do3, kall, vall, cols, vcols

    def scores(g):
        arrived(frame_copies, frame_routes, g)
        arrived(row_copies, row_routes, g)
        sums = []
        for i in range(hg):
            h = g * hg + i
            q3, do3, kall, vall, _, _ = operands(h)
            s = both_last(kall, q3)
            dp = both_last(vall, do3)
            e = jnp.exp(s * scale + bias[...])
            e_all[h] = e
            dp_all[h] = dp
            sums.append((jnp.sum(e, axis=0, keepdims=True), jnp.sum(e * dp, axis=0, keepdims=True)))
        filler = [jnp.ones((1, tokens), F32)] * (4 - hg)
        for part, (ref, index) in enumerate(((stat_send, (1, g)), (stat_own, (g,)), (stat_send, (0, g)))):
            cut = slice(part * tokens, (part + 1) * tokens)
            lines = [a[:, cut] for a, _ in sums] + filler + [b[:, cut] for _, b in sums] + filler
            ref[index] = jnp.concatenate(lines, axis=0)
        start(stat_copy, row_routes, g)

    def totals(g):
        arrived(stat_copy, row_routes, g)
        total = stat_own[g] + stat_recv[0, g] + stat_recv[1, g]
        inverse = 1.0 / total[0:4]
        coef_own[g] = jnp.concatenate([inverse, total[4:8] * inverse], axis=0)
        start(coef_copy, row_routes, g)

    def grads(g):
        arrived(coef_copy, row_routes, g)
        coef = jnp.concatenate([coef_recv[0, g], coef_own[g], coef_recv[1, g]], axis=1)
        for i in range(hg):
            h = g * hg + i
            q3, do3, kall, _, cols, vcols = operands(h)
            p = e_all[h] * coef[i : i + 1]
            half = p.astype(BF16)
            ds = (p * (dp_all[h] - coef[4 + i : 5 + i])).astype(BF16)
            dv = plain(half, do3)
            dk = plain(ds, q3) * scale
            dq = both_first(ds, kall) * scale
            for grad, where in ((dk, cols), (dv, vcols)):
                text_out[:, where] = grad[0:texts]
                dkv_send[1, :, where] = grad[texts : texts + columns].astype(BF16)
                dkv_own[:, :, where] = grad[texts + columns : texts + columns + tokens].reshape(frames, columns, HD)
                dkv_send[0, :, where] = grad[texts + columns + tokens :].astype(BF16)
            dq_send[1, :, :, cols] = dq[0:tokens].astype(BF16).reshape(frames, columns, HD)
            dq_own[:, :, cols] = dq[tokens : 2 * tokens].reshape(frames, columns, HD)
            dq_send[0, :, :, cols] = dq[2 * tokens :].astype(BF16).reshape(frames, columns, HD)
        start(dkv_copies, frame_routes, g)
        start(dq_copy, row_routes, g)

    def fold(g):
        arrived(dkv_copies, frame_routes, g)
        arrived(dq_copy, row_routes, g)
        cols = at(g)
        total = dq_own[:, :, cols] + dq_recv[0, :, :, cols].astype(F32) + dq_recv[1, :, :, cols].astype(F32)
        dq_out[:, 0, :, cols] = total.astype(BF16)
        for base in (0, width):
            where = at(g, base)
            dkv_out[0, 0, :, where] = (dkv_own[0, :, where] + dkv_recv[0, :, where].astype(F32)).astype(BF16)
            dkv_out[1 : frames - 1, 0, :, where] = dkv_own[1 : frames - 1, :, where].astype(BF16)
            dkv_out[frames - 1, 0, :, where] = (
                dkv_own[frames - 1, :, where] + dkv_recv[1, :, where].astype(F32)
            ).astype(BF16)

    def step(s, carry):
        for lag, stage in ((-AHEAD, forward), (0, scores), (LAG_TOTALS, totals), (LAG_GRADS, grads), (LAG_FOLD, fold)):

            @pl.when((s >= max(lag, 0)) & (s < groups + lag))
            def _(lag=lag, stage=stage):
                stage(s - lag)

        return carry

    lax.fori_loop(0, groups + LAG_FOLD, step, 0)

    def drain(g, carry):
        for make, routes in (
            (frame_copies, frame_routes),
            (row_copies, row_routes),
            (stat_copy, row_routes),
            (coef_copy, row_routes),
            (dkv_copies, frame_routes),
            (dq_copy, row_routes),
        ):
            sent(make, routes, g)
        return carry

    lax.fori_loop(0, groups, drain, 0)


def attention_grads(nt, nh, query, key_value, out_grad, text_kv, lanes):
    frames, _, columns, width = query.shape
    tokens = frames * columns
    texts = text_kv.shape[0]
    heads = width // HD
    groups = heads // HEADS_PER_GROUP
    keys = texts + (frames + 2) * columns
    dma = pltpu.SemaphoreType.DMA
    here = pl.BlockSpec(memory_space=pltpu.VMEM)
    away = pl.BlockSpec(memory_space=pl.ANY)
    return pl.pallas_call(
        functools.partial(attention_kernel, nt, nh),
        out_shape=(
            jax.ShapeDtypeStruct(query.shape, BF16),
            jax.ShapeDtypeStruct(key_value.shape, BF16),
            jax.ShapeDtypeStruct((texts, 2 * width), F32),
        ),
        in_specs=[away, away, away, here, here],
        out_specs=(here, here, here),
        scratch_shapes=[
            pltpu.VMEM((3, frames, columns, width), BF16),
            pltpu.VMEM((3, frames, columns, width), BF16),
            pltpu.VMEM((frames + 2, columns, 2 * width), BF16),
            pltpu.VMEM((keys, 3 * tokens), F32),
            pltpu.VMEM((heads, keys, 3 * tokens), F32),
            pltpu.VMEM((heads, keys, 3 * tokens), F32),
            pltpu.VMEM((2, groups, 8, tokens), F32),
            pltpu.VMEM((2, groups, 8, tokens), F32),
            pltpu.VMEM((groups, 8, tokens), F32),
            pltpu.VMEM((2, groups, 8, tokens), F32),
            pltpu.VMEM((groups, 8, tokens), F32),
            pltpu.VMEM((2, frames, columns, width), BF16),
            pltpu.VMEM((2, frames, columns, width), BF16),
            pltpu.VMEM((frames, columns, width), F32),
            pltpu.VMEM((2, columns, 2 * width), BF16),
            pltpu.VMEM((2, columns, 2 * width), BF16),
            pltpu.VMEM((frames, columns, 2 * width), F32),
            dma((3,)),
            dma((2, 2, groups)),
            dma((2, 2, groups)),
            dma((2, 2, groups)),
            dma((2, 2, groups)),
            dma((2, groups)),
            dma((2, groups)),
            dma((2, groups)),
            dma((2, groups)),
            dma((2, groups)),
            dma((2, groups)),
            dma((2, 2, groups)),
            dma((2, 2, groups)),
        ],
        compiler_params=pltpu.CompilerParams(collective_id=0, has_side_effects=True, vmem_limit_bytes=60 << 20),
        name="attention_grads",
    )(query, key_value, out_grad, text_kv, lanes)


def lane_limits(tile_reach, text_len, frames, columns):
    time_index, row_index = lax.axis_index("ta"), lax.axis_index("ha")
    first = time_index * frames
    padded = jnp.pad(tile_reach, ((0, 0), (1, 1), (0, 0)), constant_values=-1)
    near = lax.dynamic_slice(padded, (first, row_index, 0), (frames, 3, 2))
    away = jnp.abs(jnp.arange(3, dtype=jnp.int32) - 1)[None, :]
    reach = jnp.where(near[..., 1] >= away, near[..., 0], -1)
    reach = jnp.repeat(reach.T.reshape(-1), columns)
    length = lax.dynamic_slice(text_len, (first, row_index), (frames, 1))[:, 0]
    length = jnp.repeat(jnp.pad(length, (frames, frames)), columns)
    return jnp.stack([reach, length])


def on_device(nt, nh, query, key_value, out_grad, text_kv, tile_reach, text_len):
    lanes = lane_limits(tile_reach, text_len, query.shape[0], query.shape[2])
    query_grad, key_value_grad, text_partial = attention_grads(nt, nh, query, key_value, out_grad, text_kv, lanes)
    text_grad = lax.psum_scatter(text_partial, ("ta", "ha"), scatter_dimension=1, tiled=True).astype(BF16)
    return query_grad, key_value_grad, text_grad


def solution(mesh):
    placed = (
        P("ta", "ha", None, None),
        P("ta", "ha", None, None),
        P("ta", "ha", None, None),
        P(),
        P(),
        P(),
    )
    return jax.shard_map(
        functools.partial(on_device, mesh.shape["ta"], mesh.shape["ha"]),
        mesh=mesh,
        in_specs=placed,
        out_specs=(P("ta", "ha", None, None), P("ta", "ha", None, None), P(None, ("ta", "ha"))),
        check_vma=False,
    )
```

```python
import functools
import math

import jax
import jax.numpy as jnp
from jax import lax
from jax.experimental import pallas as pl
from jax.experimental.pallas import tpu as pltpu
from jax.sharding import PartitionSpec as P

HD = 128
MESH = pl.DeviceIdType.MESH
F32 = jnp.float32
BF16 = jnp.bfloat16

AHEAD = 2
LAG_GRADS = 1
LAG_RELAY = 2
LAG_TEXT = 2
LAG_FOLD = 4
GROUPS = 4
RUN = 8
LINES = 8


def both_last(a, b):
    return lax.dot_general(a, b, (((1,), (1,)), ((), ())), preferred_element_type=F32)


def both_first(a, b):
    return lax.dot_general(a, b, (((0,), (0,)), ((), ())), preferred_element_type=F32)


def plain(a, b):
    return lax.dot_general(a, b, (((1,), (0,)), ((), ())), preferred_element_type=F32)


def attention_kernel(
    nt,
    nh,
    q_hbm,
    kv_hbm,
    do_hbm,
    text,
    lanes,
    dq_out,
    dkv_out,
    text_out,
    q_all,
    do_all,
    kv_all,
    bias,
    e_all,
    dp_all,
    stat_send,
    near_recv,
    far_recv,
    dq_send,
    dq_recv,
    dq_own,
    dkv_send,
    dkv_recv,
    dkv_own,
    relay_kv,
    relay_dkv,
    text_part,
    core_recv,
    x_own,
    x_recv,
    y_own,
    y_recv,
    z_own,
    z_recv,
    all_recv,
    own_sem,
    row_s,
    row_r,
    fr_s,
    fr_r,
    near_s,
    near_r,
    far_s,
    far_r,
    dq_s,
    dq_r,
    dkv_s,
    dkv_r,
    relay_s,
    relay_r,
    core_s,
    core_r,
    x_s,
    x_r,
    y_s,
    y_r,
    z_s,
    z_r,
    all_s,
    all_r,
):
    frames, columns = q_all.shape[1], q_all.shape[2]
    width = q_all.shape[3]
    tokens = frames * columns
    texts = text.shape[0]
    heads = width // HD
    groups = GROUPS
    hg = heads // groups
    gw = hg * HD
    scale = 1.0 / math.sqrt(HD)
    keys = texts + (frames + 2) * columns
    ta, ha = lax.axis_index("ta"), lax.axis_index("ha")
    nx = nt // 2
    ny = nh // (2 * RUN)
    half, x = ta // nx, lax.rem(ta, nx)
    core = lax.rem(ha, 2)
    z = lax.rem(ha // 2, RUN)
    y = ha // (2 * RUN)
    first, last = nx - 1, nx
    has_dn, has_up = ha > 0, ha < nh - 1
    has_dn2, has_up2 = ha > 1, ha < nh - 2
    has_prev, has_next = ta > 0, ta < nt - 1
    dn, up = {"ha": ha - 1}, {"ha": ha + 1}
    dn2, up2 = {"ha": ha - 2}, {"ha": ha + 2}
    prev, nxt = {"ta": ta - 1}, {"ta": ta + 1}
    partner = {"ha": ha + 1 - 2 * core}

    def spot(c, yy, zz):
        return (yy * RUN + zz) * 2 + c

    own_copies = [
        pltpu.make_async_copy(q_hbm.at[:, 0], q_all.at[1], own_sem.at[0]),
        pltpu.make_async_copy(do_hbm.at[:, 0], do_all.at[1], own_sem.at[1]),
        pltpu.make_async_copy(kv_hbm.at[:, 0], kv_all.at[pl.ds(1, frames)], own_sem.at[2]),
    ]
    for copy in own_copies:
        copy.start()

    always = ta >= 0
    x_peers = [lax.rem(x + d, nx) for d in range(1, nx)]
    y_peers = [lax.rem(y + d, ny) for d in range(1, ny)]
    all_peers = [(core, yy) for yy in y_peers] + [(1 - core, lax.rem(y + d, ny)) for d in range(ny)]
    z_here = half * RUN + z
    z_peers = [lax.rem(z_here + d, 2 * RUN) for d in range(1, 2 * RUN)]
    greet = [(has_dn, dn), (has_up, up), (has_dn2, dn2), (has_up2, up2)]
    greet += [(always, {"ta": half * nx + xx}) for xx in x_peers]
    greet += [(always, {"ha": spot(c, yy, z)}) for c, yy in all_peers]
    greet += [(always, {"ta": (p // RUN) * nx + x, "ha": spot(core, y, lax.rem(p, RUN))}) for p in z_peers]
    greet += [(ta == first, {"ta": nx + j}) for j in range(nx)]
    greet += [(ta == last, {"ta": j}) for j in range(nx)]
    greet += [(ta < first, {"ta": last}), (ta > last, {"ta": first})]
    barrier = pltpu.get_barrier_semaphore()
    for has, where in greet:

        @pl.when(has)
        def _(where=where):
            pl.semaphore_signal(barrier, inc=1, device_id=where, device_id_type=MESH)

    pl.semaphore_wait(barrier, sum(has.astype(jnp.int32) for has, _ in greet))

    def at(g, base=0):
        return pl.ds(pl.multiple_of(base + g * gw, HD), gw)

    def remote(src, dst, send, recv, where):
        return pltpu.make_async_remote_copy(
            src_ref=src,
            dst_ref=dst,
            send_sem=send,
            recv_sem=recv,
            device_id=where,
            device_id_type=MESH,
        )

    def row_copies(g, side, where):
        slot = 0 if side == 0 else 2
        return [
            remote(
                hbm.at[:, 0, :, at(g)], ref.at[slot, :, :, at(g)], row_s.at[side, i, g], row_r.at[side, i, g], where
            )
            for i, (hbm, ref) in enumerate(((q_hbm, q_all), (do_hbm, do_all)))
        ]

    bases = (0, width)

    def kv_source(g, side, base):
        return kv_hbm.at[frames - 1 if side == 0 else 0, 0, :, at(g, base)]

    def kv_target(g, side, base):
        return kv_all.at[0 if side == 0 else frames + 1, :, at(g, base)]

    def dkv_source(g, side, base):
        return dkv_send.at[side, :, at(g, base)]

    def dkv_target(g, side, base):
        return dkv_recv.at[side, :, at(g, base)]

    def frame_copies(g, side, where):
        return [
            remote(
                kv_source(g, side, base), kv_target(g, side, base), fr_s.at[side, i, g], fr_r.at[side, i, g], where
            )
            for i, base in enumerate(bases)
        ]

    def dkv_copies(g, side, where):
        return [
            remote(
                dkv_source(g, side, base), dkv_target(g, side, base), dkv_s.at[side, i, g], dkv_r.at[side, i, g], where
            )
            for i, base in enumerate(bases)
        ]

    def to_relay(kind, g, side, where):
        source, send, held = ((kv_source, fr_s, relay_kv), (dkv_source, dkv_s, relay_dkv))[kind]
        return [
            remote(source(g, side, base), held.at[i], send.at[side, i, g], relay_r.at[kind, i], where)
            for i, base in enumerate(bases)
        ]

    def from_relay(kind, g, side, where):
        held, target, recv = ((relay_kv, kv_target, fr_r), (relay_dkv, dkv_target, dkv_r))[kind]
        return [
            remote(held.at[i], target(g, side, base), relay_s.at[kind, i], recv.at[side, i, g], where)
            for i, base in enumerate(bases)
        ]

    def near_copy(g, side, where):
        return [remote(stat_send.at[side, g], near_recv.at[side, g], near_s.at[side, g], near_r.at[side, g], where)]

    def far_copy(g, side, where):
        return [remote(stat_send.at[side, g, 0], far_recv.at[side, g], far_s.at[side, g], far_r.at[side, g], where)]

    def dq_copy(g, side, where):
        return [
            remote(
                dq_send.at[side, :, :, at(g)], dq_recv.at[side, :, :, at(g)], dq_s.at[side, g], dq_r.at[side, g], where
            )
        ]

    row_routes = ((0, has_up, up, has_dn), (1, has_dn, dn, has_up))
    far_routes = ((0, has_up2, up2, has_dn2), (1, has_dn2, dn2, has_up2))
    frame_routes = ((0, has_next, nxt, has_prev), (1, has_prev, prev, has_next))
    crossings = ((0, ta == first, nxt), (1, ta == last, prev))

    def start(make, routes, g):
        for side, has, where, _ in routes:

            @pl.when(has)
            def _(side=side, where=where):
                for copy in make(g, side, where):
                    copy.start()

    def arrived(make, routes, g):
        for side, _, where, has in routes:

            @pl.when(has)
            def _(side=side, where=where):
                for copy in make(g, side, where):
                    copy.wait_recv()

    def sent(make, routes, g):
        for side, has, where, _ in routes:

            @pl.when(has)
            def _(side=side, where=where):
                for copy in make(g, side, where):
                    copy.wait_send()

    def start_frames(kind, g):
        make = (frame_copies, dkv_copies)[kind]
        for (side, has, where, _), (_, crosses, _) in zip(frame_routes, crossings):
            relayed = crosses & (g != x)

            @pl.when(has & jnp.logical_not(relayed))
            def _(side=side, where=where):
                for copy in make(g, side, where):
                    copy.start()

            @pl.when(relayed)
            def _(side=side):
                for copy in to_relay(kind, g, side, {"ta": half * nx + g}):
                    copy.start()

    relays = ((0, (half == 0) & (ta != first), {"ta": last}), (1, (half == 1) & (ta != last), {"ta": first}))

    def pass_on(kind):
        for side, has, where in relays:

            @pl.when(has)
            def _(side=side, where=where):
                for copy in to_relay(kind, x, side, where):
                    copy.wait_recv()
                for copy in from_relay(kind, x, side, where):
                    copy.start()

    def passed_on(kind):
        for side, has, where in relays:

            @pl.when(has)
            def _(side=side, where=where):
                for copy in from_relay(kind, x, side, where):
                    copy.wait_send()

    def forward(g):
        start(row_copies, row_routes, g)

    for g in range(groups):
        start_frames(0, g)
    for g in range(AHEAD):
        forward(g)

    for side, _, _, has in row_routes:

        @pl.when(jnp.logical_not(has))
        def _(side=side):
            slot = 0 if side == 0 else 2
            q_all[slot] = jnp.zeros(q_all.shape[1:], BF16)
            do_all[slot] = jnp.zeros(do_all.shape[1:], BF16)
            near_recv[side, :, 0] = jnp.zeros((groups,) + near_recv.shape[3:], F32)
            near_recv[side, :, 1] = jnp.ones((groups,) + near_recv.shape[3:], F32)
            dq_recv[side] = jnp.zeros(dq_recv.shape[1:], BF16)

    for side, _, _, has in far_routes:

        @pl.when(jnp.logical_not(has))
        def _(side=side):
            far_recv[side] = jnp.zeros(far_recv.shape[1:], F32)

    for side, _, _, has in frame_routes:

        @pl.when(jnp.logical_not(has))
        def _(side=side):
            slot = 0 if side == 0 else frames + 1
            kv_all[slot] = jnp.zeros(kv_all.shape[1:], BF16)
            dkv_recv[side] = jnp.zeros(dkv_recv.shape[1:], BF16)

    line = lax.broadcasted_iota(jnp.int32, (keys, 3 * tokens), 0)
    lane = lax.broadcasted_iota(jnp.int32, (keys, 3 * tokens), 1)
    query_frame = lax.rem(lane, tokens) // columns
    key_frame = (line - texts + columns) // columns - 2
    gap = jnp.abs(key_frame - query_frame)
    inside = ((key_frame >= 0) | has_prev) & ((key_frame < frames) | has_next)
    latent_seen = (line >= texts) & inside & (gap <= lanes[0:1, :])
    text_seen = (line < texts) & (line < lanes[1:2, :])
    bias[...] = jnp.where(latent_seen | text_seen, 0.0, -1e30)
    pass_on(0)
    for copy in own_copies:
        copy.wait()

    def operands(h):
        cols = pl.ds(pl.multiple_of(h * HD, HD), HD)
        vcols = pl.ds(pl.multiple_of(width + h * HD, HD), HD)
        q3 = q_all[:, :, :, cols].reshape(3 * tokens, HD)
        do3 = do_all[:, :, :, cols].reshape(3 * tokens, HD)
        kall = jnp.concatenate([text[:, cols], kv_all[:, :, cols].reshape(-1, HD)], axis=0)
        vall = jnp.concatenate([text[:, vcols], kv_all[:, :, vcols].reshape(-1, HD)], axis=0)
        return q3, do3, kall, vall, cols, vcols

    def scores(g):
        arrived(frame_copies, frame_routes, g)
        arrived(row_copies, row_routes, g)
        sums = []
        for i in range(hg):
            h = g * hg + i
            q3, do3, kall, vall, _, _ = operands(h)
            s = both_last(kall, q3)
            dp = both_last(vall, do3)
            e = jnp.exp(s * scale + bias[...])
            e_all[h] = e
            dp_all[h] = dp
            sums.append((jnp.sum(e, axis=0, keepdims=True), jnp.sum(e * dp, axis=0, keepdims=True)))
        filler = [jnp.ones((1, tokens), F32)] * (LINES - hg)
        blocks = []
        for part in range(3):
            cut = slice(part * tokens, (part + 1) * tokens)
            lines = [a[:, cut] for a, _ in sums] + filler + [b[:, cut] for _, b in sums] + filler
            blocks.append(jnp.concatenate(lines, axis=0))
        stat_send[0, g, 0] = blocks[2]
        stat_send[1, g, 0] = blocks[0]
        stat_send[0, g, 1] = blocks[1]
        stat_send[1, g, 1] = blocks[1]
        start(near_copy, row_routes, g)
        start(far_copy, far_routes, g)

    def grads(g):
        arrived(near_copy, row_routes, g)
        arrived(far_copy, far_routes, g)
        total = jnp.concatenate(
            [
                stat_send[1, g, 0] + near_recv[0, g, 1] + far_recv[0, g],
                stat_send[0, g, 1] + near_recv[0, g, 0] + near_recv[1, g, 0],
                stat_send[0, g, 0] + near_recv[1, g, 1] + far_recv[1, g],
            ],
            axis=1,
        )
        inverse = 1.0 / total[0:LINES]
        delta = total[LINES:] * inverse
        for i in range(hg):
            h = g * hg + i
            q3, do3, kall, _, cols, vcols = operands(h)
            p = e_all[h] * inverse[i : i + 1]
            weight = p.astype(BF16)
            ds = (p * (dp_all[h] - delta[i : i + 1])).astype(BF16)
            dv = plain(weight, do3)
            dk = plain(ds, q3) * scale
            dq = both_first(ds, kall) * scale
            for kind, (grad, where) in enumerate(((dk, cols), (dv, vcols))):
                for part in range(2):
                    cut = slice(part * (texts // 2), (part + 1) * (texts // 2))
                    text_part[g, part, kind, :, i * HD : (i + 1) * HD] = grad[cut]
                dkv_send[1, :, where] = grad[texts : texts + columns].astype(BF16)
                dkv_own[:, :, where] = grad[texts + columns : texts + columns + tokens].reshape(frames, columns, HD)
                dkv_send[0, :, where] = grad[texts + columns + tokens :].astype(BF16)
            dq_send[1, :, :, cols] = dq[0:tokens].astype(BF16).reshape(frames, columns, HD)
            dq_own[:, :, cols] = dq[tokens : 2 * tokens].reshape(frames, columns, HD)
            dq_send[0, :, :, cols] = dq[2 * tokens :].astype(BF16).reshape(frames, columns, HD)
        core_copy(g).start()
        start_frames(1, g)
        start(dq_copy, row_routes, g)

    def core_copy(g):
        return remote(text_part.at[g, 1 - core], core_recv.at[g], core_s.at[g], core_r.at[g], partner)

    def x_copy(g, source):
        return remote(x_own.at[g], x_recv.at[source], x_s.at[g], x_r.at[source], {"ta": half * nx + g})

    def y_copy(target, source, i):
        return remote(y_own.at[target], y_recv.at[source], y_s.at[i], y_r.at[source], {"ha": spot(core, target, z)})

    def z_copy(target, source, i):
        where = {"ta": (target // RUN) * nx + x, "ha": spot(core, y, lax.rem(target, RUN))}
        return remote(z_own.at[target // RUN], z_recv.at[source], z_s.at[i], z_r.at[source], where)

    def all_copy(c, yy, source, i):
        mine = core * ny + y
        return remote(all_recv.at[mine], all_recv.at[mine], all_s.at[i], all_r.at[source], {"ha": spot(c, yy, z)})

    def text_over_cores(g):
        core_copy(g).wait_recv()
        x_own[g] = text_part[g, core] + core_recv[g]

        @pl.when(g != x)
        def _():
            x_copy(g, x).start()

    def text_over_x(g):
        @pl.when(g == x)
        def _():
            total = x_own[x]
            for source in x_peers:
                x_copy(x, source).wait_recv()
                total = total + x_recv[source]
            part = total.shape[1] // ny
            for target in range(ny):
                y_own[target] = total[:, target * part : (target + 1) * part]
            for i, target in enumerate(y_peers):
                y_copy(target, y, i).start()

    def text_over_y(g):
        @pl.when(g == x)
        def _():
            total = y_own[y]
            for i, source in enumerate(y_peers):
                y_copy(source, source, i).wait_recv()
                total = total + y_recv[source]
            z_own[...] = total
            for i, target in enumerate(z_peers):
                z_copy(target, z_here, i).start()

    def text_over_z(g):
        @pl.when(g == x)
        def _():
            total = z_own[half]
            for i, source in enumerate(z_peers):
                z_copy(source, source, i).wait_recv()
                total = total + z_recv[source]
            all_recv[core * ny + y] = total
            for i, (c, yy) in enumerate(all_peers):
                all_copy(c, yy, core * ny + y, i).start()

    def text_done(g):
        @pl.when(g == x)
        def _():
            for i, (c, yy) in enumerate(all_peers):
                remote(
                    all_recv.at[c * ny + yy],
                    all_recv.at[c * ny + yy],
                    all_s.at[i],
                    all_r.at[c * ny + yy],
                    {"ha": spot(c, yy, z)},
                ).wait_recv()
            text_out[...] = all_recv[...]

    def text_sent():
        for g in range(groups):
            core_copy(g).wait_send()

            @pl.when(g != x)
            def _(g=g):
                x_copy(g, x).wait_send()

        for i, target in enumerate(y_peers):
            y_copy(target, y, i).wait_send()
        for i, target in enumerate(z_peers):
            z_copy(target, z_here, i).wait_send()
        for i, (c, yy) in enumerate(all_peers):
            all_copy(c, yy, core * ny + y, i).wait_send()

    def relay(g):
        @pl.when(g == x)
        def _():
            pass_on(1)

    def fold(g):
        arrived(dkv_copies, frame_routes, g)
        arrived(dq_copy, row_routes, g)
        cols = at(g)
        total = dq_own[:, :, cols] + dq_recv[0, :, :, cols].astype(F32) + dq_recv[1, :, :, cols].astype(F32)
        dq_out[:, 0, :, cols] = total.astype(BF16)
        for base in bases:
            where = at(g, base)
            dkv_out[0, 0, :, where] = (dkv_own[0, :, where] + dkv_recv[0, :, where].astype(F32)).astype(BF16)
            dkv_out[1 : frames - 1, 0, :, where] = dkv_own[1 : frames - 1, :, where].astype(BF16)
            dkv_out[frames - 1, 0, :, where] = (
                dkv_own[frames - 1, :, where] + dkv_recv[1, :, where].astype(F32)
            ).astype(BF16)

    stages = (
        (0, scores),
        (-AHEAD, forward),
        (LAG_GRADS, grads),
        (LAG_RELAY, relay),
        (LAG_TEXT, text_over_cores),
        (LAG_TEXT + 1, text_over_x),
        (LAG_TEXT + 2, text_over_y),
        (LAG_FOLD, fold),
        (LAG_TEXT + 3, text_over_z),
        (LAG_TEXT + 4, text_done),
    )

    def step(s, carry):
        for lag, stage in stages:

            @pl.when((s >= max(lag, 0)) & (s < groups + lag))
            def _(lag=lag, stage=stage):
                stage(s - lag)

        return carry

    lax.fori_loop(0, groups + LAG_TEXT + 4, step, 0)

    def drain(g, carry):
        for make, routes in (
            (frame_copies, frame_routes),
            (row_copies, row_routes),
            (near_copy, row_routes),
            (far_copy, far_routes),
            (dkv_copies, frame_routes),
            (dq_copy, row_routes),
        ):
            sent(make, routes, g)
        return carry

    lax.fori_loop(0, groups, drain, 0)
    passed_on(0)
    passed_on(1)
    text_sent()


def attention_grads(nt, nh, query, key_value, out_grad, text_kv, lanes):
    frames, _, columns, width = query.shape
    tokens = frames * columns
    texts = text_kv.shape[0]
    heads = width // HD
    groups = GROUPS
    gw = width // groups
    nx, ny = nt // 2, nh // (2 * RUN)
    keys = texts + (frames + 2) * columns
    dma = pltpu.SemaphoreType.DMA
    here = pl.BlockSpec(memory_space=pltpu.VMEM)
    away = pl.BlockSpec(memory_space=pl.ANY)
    return pl.pallas_call(
        functools.partial(attention_kernel, nt, nh),
        out_shape=(
            jax.ShapeDtypeStruct(query.shape, BF16),
            jax.ShapeDtypeStruct(key_value.shape, BF16),
            jax.ShapeDtypeStruct((2 * ny, texts // (2 * ny), gw), F32),
        ),
        in_specs=[away, away, away, here, here],
        out_specs=(here, here, here),
        scratch_shapes=[
            pltpu.VMEM((3, frames, columns, width), BF16),
            pltpu.VMEM((3, frames, columns, width), BF16),
            pltpu.VMEM((frames + 2, columns, 2 * width), BF16),
            pltpu.VMEM((keys, 3 * tokens), F32),
            pltpu.VMEM((heads, keys, 3 * tokens), F32),
            pltpu.VMEM((heads, keys, 3 * tokens), F32),
            pltpu.VMEM((2, groups, 2, 2 * LINES, tokens), F32),
            pltpu.VMEM((2, groups, 2, 2 * LINES, tokens), F32),
            pltpu.VMEM((2, groups, 2 * LINES, tokens), F32),
            pltpu.VMEM((2, frames, columns, width), BF16),
            pltpu.VMEM((2, frames, columns, width), BF16),
            pltpu.VMEM((frames, columns, width), F32),
            pltpu.VMEM((2, columns, 2 * width), BF16),
            pltpu.VMEM((2, columns, 2 * width), BF16),
            pltpu.VMEM((frames, columns, 2 * width), F32),
            pltpu.VMEM((2, columns, gw), BF16),
            pltpu.VMEM((2, columns, gw), BF16),
            pltpu.VMEM((groups, 2, 2, texts // 2, gw), F32),
            pltpu.VMEM((groups, 2, texts // 2, gw), F32),
            pltpu.VMEM((groups, 2, texts // 2, gw), F32),
            pltpu.VMEM((nx, 2, texts // 2, gw), F32),
            pltpu.VMEM((ny, 2, texts // (2 * ny), gw), F32),
            pltpu.VMEM((ny, 2, texts // (2 * ny), gw), F32),
            pltpu.VMEM((2, texts // (2 * ny), gw), F32),
            pltpu.VMEM((2 * RUN, texts // (2 * ny), gw), F32),
            pltpu.VMEM((2 * ny, texts // (2 * ny), gw), F32),
            dma((3,)),
            dma((2, 2, groups)),
            dma((2, 2, groups)),
            dma((2, 2, groups)),
            dma((2, 2, groups)),
            dma((2, groups)),
            dma((2, groups)),
            dma((2, groups)),
            dma((2, groups)),
            dma((2, groups)),
            dma((2, groups)),
            dma((2, 2, groups)),
            dma((2, 2, groups)),
            dma((2, 2)),
            dma((2, 2)),
            dma((groups,)),
            dma((groups,)),
            dma((groups,)),
            dma((nx,)),
            dma((ny,)),
            dma((ny,)),
            dma((2 * RUN,)),
            dma((2 * RUN,)),
            dma((2 * ny,)),
            dma((2 * ny,)),
        ],
        compiler_params=pltpu.CompilerParams(collective_id=0, has_side_effects=True, vmem_limit_bytes=60 << 20),
        name="attention_grads",
    )(query, key_value, out_grad, text_kv, lanes)


def lane_limits(tile_reach, text_len, frames, columns):
    time_index, row_index = lax.axis_index("ta"), lax.axis_index("ha")
    first = time_index * frames
    padded = jnp.pad(tile_reach, ((0, 0), (1, 1), (0, 0)), constant_values=-1)
    near = lax.dynamic_slice(padded, (first, row_index, 0), (frames, 3, 2))
    away = jnp.abs(jnp.arange(3, dtype=jnp.int32) - 1)[None, :]
    reach = jnp.where(near[..., 1] >= away, near[..., 0], -1)
    reach = jnp.repeat(reach.T.reshape(-1), columns)
    length = lax.dynamic_slice(text_len, (first, row_index), (frames, 1))[:, 0]
    length = jnp.repeat(jnp.pad(length, (frames, frames)), columns)
    return jnp.stack([reach, length])


def on_device(nt, nh, query, key_value, out_grad, text_kv, tile_reach, text_len):
    lanes = lane_limits(tile_reach, text_len, query.shape[0], query.shape[2])
    query_grad, key_value_grad, text_partial = attention_grads(nt, nh, query, key_value, out_grad, text_kv, lanes)
    share = text_kv.shape[1] // (nt * nh)
    lines = text_partial.reshape(text_kv.shape[0], -1)
    text_grad = lax.dynamic_slice_in_dim(lines, lax.axis_index("ha") * share, share, axis=1).astype(BF16)
    return query_grad, key_value_grad, text_grad


def solution(mesh):
    placed = (
        P("ta", "ha", None, None),
        P("ta", "ha", None, None),
        P("ta", "ha", None, None),
        P(),
        P(),
        P(),
    )
    return jax.shard_map(
        functools.partial(on_device, mesh.shape["ta"], mesh.shape["ha"]),
        mesh=mesh,
        in_specs=placed,
        out_specs=(P("ta", "ha", None, None), P("ta", "ha", None, None), P(None, ("ta", "ha"))),
        check_vma=False,
    )
```

```python
import functools
import math

import jax
import jax.numpy as jnp
from jax import lax
from jax.experimental import pallas as pl
from jax.experimental.pallas import tpu as pltpu
from jax.sharding import PartitionSpec as P

HD = 128
MESH = pl.DeviceIdType.MESH
F32 = jnp.float32
BF16 = jnp.bfloat16

CHUNKS = (5, 5, 5, 5)
AHEAD = 2
FIRST = 1
LIMIT = 60
LAG_FOLD = 4
BLOCKS = 4
RUN = 8
LINES = 8


def both_last(a, b):
    return lax.dot_general(a, b, (((1,), (1,)), ((), ())), preferred_element_type=F32)


def both_first(a, b):
    return lax.dot_general(a, b, (((0,), (0,)), ((), ())), preferred_element_type=F32)


def plain(a, b):
    return lax.dot_general(a, b, (((1,), (0,)), ((), ())), preferred_element_type=F32)


def attention_kernel(
    nt,
    nh,
    q_hbm,
    kv_hbm,
    do_hbm,
    text,
    reach,
    length,
    dq_out,
    dkv_out,
    text_out,
    q_all,
    do_all,
    kv_all,
    bias,
    e_all,
    dp_all,
    ds_all,
    stat_send,
    near_recv,
    far_recv,
    dq_send,
    dq_recv,
    dq_own,
    dkv_send,
    dkv_recv,
    dkv_own,
    relay_kv,
    relay_dkv,
    text_part,
    core_recv,
    xy_own,
    xy_recv,
    z_own,
    z_recv,
    all_own,
    all_recv,
    own_sem,
    row_s,
    row_r,
    fr_s,
    fr_r,
    near_s,
    near_r,
    far_s,
    far_r,
    dq_s,
    dq_r,
    dkv_s,
    dkv_r,
    relay_s,
    relay_r,
    core_s,
    core_r,
    xy_s,
    xy_r,
    z_s,
    z_r,
    all_s,
    all_r,
):
    frames, columns = q_all.shape[1], q_all.shape[2]
    width = q_all.shape[3]
    tokens = frames * columns
    texts = text.shape[0]
    heads = width // HD
    starts = [sum(CHUNKS[:c]) for c in range(len(CHUNKS) + 1)]
    hb = heads // BLOCKS
    bw = hb * HD
    scale = 1.0 / math.sqrt(HD)
    keys = texts + (frames + 2) * columns
    ta, ha = lax.axis_index("ta"), lax.axis_index("ha")
    nx = nt // 2
    ny = nh // (2 * RUN)
    half, x = ta // nx, lax.rem(ta, nx)
    core = lax.rem(ha, 2)
    z = lax.rem(ha // 2, RUN)
    y = ha // (2 * RUN)
    first, last = nx - 1, nx
    has_dn, has_up = ha > 0, ha < nh - 1
    has_dn2, has_up2 = ha > 1, ha < nh - 2
    has_prev, has_next = ta > 0, ta < nt - 1
    dn, up = {"ha": ha - 1}, {"ha": ha + 1}
    dn2, up2 = {"ha": ha - 2}, {"ha": ha + 2}
    prev, nxt = {"ta": ta - 1}, {"ta": ta + 1}
    partner = {"ha": ha + 1 - 2 * core}

    def spot(c, yy, zz):
        return (yy * RUN + zz) * 2 + c

    own_copies = [
        pltpu.make_async_copy(q_hbm.at[:, 0], q_all.at[1], own_sem.at[0]),
        pltpu.make_async_copy(do_hbm.at[:, 0], do_all.at[1], own_sem.at[1]),
        pltpu.make_async_copy(kv_hbm.at[:, 0], kv_all.at[pl.ds(1, frames)], own_sem.at[2]),
    ]
    for copy in own_copies:
        copy.start()

    always = ta >= 0
    x_peers = [lax.rem(x + d, nx) for d in range(1, nx)]
    y_peers = [lax.rem(y + d, ny) for d in range(1, ny)]
    xy_peers = [(x, yy) for yy in y_peers] + [(xx, lax.rem(y + d, ny)) for xx in x_peers for d in range(ny)]
    near_peers = [(core, xx, yy) for xx, yy in xy_peers]
    near_peers += [(1 - core, xx, lax.rem(y + d, ny)) for xx in [x] + x_peers for d in range(ny)]
    z_here = half * RUN + z
    z_peers = [lax.rem(z_here + d, 2 * RUN) for d in range(1, 2 * RUN)]
    greet = [(has_dn, dn), (has_up, up), (has_dn2, dn2), (has_up2, up2)]
    greet += [(always, {"ta": half * nx + xx, "ha": spot(c, yy, z)}) for c, xx, yy in near_peers]
    greet += [(always, {"ta": (p // RUN) * nx + x, "ha": spot(core, y, lax.rem(p, RUN))}) for p in z_peers]
    greet += [(ta == first, {"ta": nx + j}) for j in range(nx)]
    greet += [(ta == last, {"ta": j}) for j in range(nx)]
    greet += [(ta < first, {"ta": last}), (ta > last, {"ta": first})]
    barrier = pltpu.get_barrier_semaphore()
    for has, where in greet:

        @pl.when(has)
        def _(where=where):
            pl.semaphore_signal(barrier, inc=1, device_id=where, device_id_type=MESH)

    place = ta * frames
    near_reach = reach[pl.ds(place, frames)].astype(F32)
    near_length = length[pl.ds(pl.multiple_of(place, frames), frames), :].astype(F32)
    token_frame = lax.broadcasted_iota(jnp.int32, (1, tokens), 1) // columns
    row_of = lax.broadcasted_iota(jnp.int32, near_reach.shape, 2)
    pieces = []
    for j, has in ((0, has_dn), (1, always), (2, has_up)):
        found = jnp.sum(jnp.where(row_of == ha + j - 1, near_reach, 0.0), axis=2)
        piece = jnp.full((1, tokens), -1.0, F32)
        for f in range(frames):
            shown = (found[f : f + 1, 1:2] >= abs(j - 1)) & has
            piece = jnp.where((token_frame == f) & shown, found[f : f + 1, 0:1], piece)
        pieces.append(piece)
    limit = jnp.concatenate(pieces, axis=1)
    found = jnp.sum(
        jnp.where(lax.broadcasted_iota(jnp.int32, near_length.shape, 1) == ha, near_length, 0.0), axis=1, keepdims=True
    )
    shown = jnp.zeros((1, tokens), F32)
    for f in range(frames):
        shown = jnp.where(token_frame == f, found[f : f + 1], shown)
    text_limit = jnp.concatenate([jnp.zeros((1, tokens), F32), shown, jnp.zeros((1, tokens), F32)], axis=1)
    line = lax.broadcasted_iota(jnp.int32, (keys, 3 * tokens), 0)
    lane = lax.broadcasted_iota(jnp.int32, (keys, 3 * tokens), 1)
    query_frame = lax.rem(lane, tokens) // columns
    key_frame = (line - texts + columns) // columns - 2
    gap = jnp.abs(key_frame - query_frame).astype(F32)
    inside = ((key_frame >= 0) | has_prev) & ((key_frame < frames) | has_next)
    latent_seen = (line >= texts) & inside & (gap <= limit)
    text_seen = (line < texts) & (line.astype(F32) < text_limit)
    bias[...] = jnp.where(latent_seen | text_seen, 0.0, -1e30)

    pl.semaphore_wait(barrier, sum(has.astype(jnp.int32) for has, _ in greet))

    def at(c):
        return pl.ds(starts[c] * HD, CHUNKS[c] * HD)

    def of(b, base=0):
        return pl.ds(pl.multiple_of(base + b * bw, HD), bw)

    def remote(src, dst, send, recv, where):
        return pltpu.make_async_remote_copy(
            src_ref=src,
            dst_ref=dst,
            send_sem=send,
            recv_sem=recv,
            device_id=where,
            device_id_type=MESH,
        )

    def row_copies(g, side, where):
        slot = 0 if side == 0 else 2
        return [
            remote(
                hbm.at[:, 0, :, at(g)], ref.at[slot, :, :, at(g)], row_s.at[side, i, g], row_r.at[side, i, g], where
            )
            for i, (hbm, ref) in enumerate(((q_hbm, q_all), (do_hbm, do_all)))
        ]

    bases = (0, width)

    def kv_source(g, side, base):
        return kv_hbm.at[frames - 1 if side == 0 else 0, 0, :, of(g, base)]

    def kv_target(g, side, base):
        return kv_all.at[0 if side == 0 else frames + 1, :, of(g, base)]

    def dkv_source(g, side, base):
        return dkv_send.at[side, :, of(g, base)]

    def dkv_target(g, side, base):
        return dkv_recv.at[side, :, of(g, base)]

    def frame_copies(g, side, where):
        return [
            remote(
                kv_source(g, side, base), kv_target(g, side, base), fr_s.at[side, i, g], fr_r.at[side, i, g], where
            )
            for i, base in enumerate(bases)
        ]

    def dkv_copies(g, side, where):
        return [
            remote(
                dkv_source(g, side, base), dkv_target(g, side, base), dkv_s.at[side, i, g], dkv_r.at[side, i, g], where
            )
            for i, base in enumerate(bases)
        ]

    def to_relay(kind, g, side, where):
        source, send, held = ((kv_source, fr_s, relay_kv), (dkv_source, dkv_s, relay_dkv))[kind]
        return [
            remote(source(g, side, base), held.at[i], send.at[side, i, g], relay_r.at[kind, i], where)
            for i, base in enumerate(bases)
        ]

    def from_relay(kind, g, side, where):
        held, target, recv = ((relay_kv, kv_target, fr_r), (relay_dkv, dkv_target, dkv_r))[kind]
        return [
            remote(held.at[i], target(g, side, base), relay_s.at[kind, i], recv.at[side, i, g], where)
            for i, base in enumerate(bases)
        ]

    def near_copy(g, side, where):
        return [remote(stat_send.at[side, g], near_recv.at[side, g], near_s.at[side, g], near_r.at[side, g], where)]

    def far_copy(g, side, where):
        return [remote(stat_send.at[side, g, 0], far_recv.at[side, g], far_s.at[side, g], far_r.at[side, g], where)]

    def dq_copy(g, side, where):
        return [
            remote(
                dq_send.at[side, :, :, at(g)], dq_recv.at[side, :, :, at(g)], dq_s.at[side, g], dq_r.at[side, g], where
            )
        ]

    row_routes = ((0, has_up, up, has_dn), (1, has_dn, dn, has_up))
    far_routes = ((0, has_up2, up2, has_dn2), (1, has_dn2, dn2, has_up2))
    frame_routes = ((0, has_next, nxt, has_prev), (1, has_prev, prev, has_next))
    crossings = ((0, ta == first, nxt), (1, ta == last, prev))

    def start(make, routes, g):
        for side, has, where, _ in routes:

            @pl.when(has)
            def _(side=side, where=where):
                for copy in make(g, side, where):
                    copy.start()

    def arrived(make, routes, g):
        for side, _, where, has in routes:

            @pl.when(has)
            def _(side=side, where=where):
                for copy in make(g, side, where):
                    copy.wait_recv()

    def sent(make, routes, g):
        for side, has, where, _ in routes:

            @pl.when(has)
            def _(side=side, where=where):
                for copy in make(g, side, where):
                    copy.wait_send()

    def start_frames(kind, g):
        make = (frame_copies, dkv_copies)[kind]
        for (side, has, where, _), (_, crosses, _) in zip(frame_routes, crossings):
            relayed = crosses & (g != x)

            @pl.when(has & jnp.logical_not(relayed))
            def _(side=side, where=where):
                for copy in make(g, side, where):
                    copy.start()

            @pl.when(relayed)
            def _(side=side):
                for copy in to_relay(kind, g, side, {"ta": half * nx + g}):
                    copy.start()

    relays = ((0, (half == 0) & (ta != first), {"ta": last}), (1, (half == 1) & (ta != last), {"ta": first}))

    def pass_on(kind):
        for side, has, where in relays:

            @pl.when(has)
            def _(side=side, where=where):
                for copy in to_relay(kind, x, side, where):
                    copy.wait_recv()
                for copy in from_relay(kind, x, side, where):
                    copy.start()

    def passed_on(kind):
        for side, has, where in relays:

            @pl.when(has)
            def _(side=side, where=where):
                for copy in from_relay(kind, x, side, where):
                    copy.wait_send()

    def forward(g):
        start(row_copies, row_routes, g)

    for b in range(BLOCKS):
        start_frames(0, b)
    for g in range(FIRST):
        forward(g)

    for side, _, _, has in row_routes:

        @pl.when(jnp.logical_not(has))
        def _(side=side):
            slot = 0 if side == 0 else 2
            q_all[slot] = jnp.zeros(q_all.shape[1:], BF16)
            do_all[slot] = jnp.zeros(do_all.shape[1:], BF16)
            near_recv[side, :, 0] = jnp.zeros((len(CHUNKS),) + near_recv.shape[3:], F32)
            near_recv[side, :, 1] = jnp.ones((len(CHUNKS),) + near_recv.shape[3:], F32)
            dq_recv[side] = jnp.zeros(dq_recv.shape[1:], BF16)

    for side, _, _, has in far_routes:

        @pl.when(jnp.logical_not(has))
        def _(side=side):
            far_recv[side] = jnp.zeros(far_recv.shape[1:], F32)

    for side, _, _, has in frame_routes:

        @pl.when(jnp.logical_not(has))
        def _(side=side):
            slot = 0 if side == 0 else frames + 1
            kv_all[slot] = jnp.zeros(kv_all.shape[1:], BF16)
            dkv_recv[side] = jnp.zeros(dkv_recv.shape[1:], BF16)

    pass_on(0)
    for g in range(FIRST, AHEAD):
        forward(g)
    for copy in own_copies:
        copy.wait()

    def operands(h):
        cols, vcols = pl.ds(h * HD, HD), pl.ds(width + h * HD, HD)
        q3 = q_all[:, :, :, cols].reshape(3 * tokens, HD)
        do3 = do_all[:, :, :, cols].reshape(3 * tokens, HD)
        kall = jnp.concatenate([text[:, cols], kv_all[:, :, cols].reshape(-1, HD)], axis=0)
        vall = jnp.concatenate([text[:, vcols], kv_all[:, :, vcols].reshape(-1, HD)], axis=0)
        return q3, do3, kall, vall, cols, vcols

    def finished(g):
        return [b for b in range(BLOCKS) if starts[g] < (b + 1) * hb <= starts[g + 1]]

    def scores(g):
        for b in range(BLOCKS):
            if starts[g] <= b * hb < starts[g + 1]:
                arrived(frame_copies, frame_routes, b)
        arrived(row_copies, row_routes, g)
        sums = []
        hg = CHUNKS[g]
        for h in range(starts[g], starts[g + 1]):
            q3, do3, kall, vall, _, _ = operands(h)
            s = both_last(kall, q3)
            dp = both_last(vall, do3)
            e = jnp.exp(s * scale + bias[...])
            e_all[h] = e
            dp_all[h] = dp
            sums.append((jnp.sum(e, axis=0, keepdims=True), jnp.sum(e * dp, axis=0, keepdims=True)))
        filler = [jnp.ones((1, tokens), F32)] * (LINES - hg)
        blocks = []
        for part in range(3):
            cut = slice(part * tokens, (part + 1) * tokens)
            lines = [a[:, cut] for a, _ in sums] + filler + [b[:, cut] for _, b in sums] + filler
            blocks.append(jnp.concatenate(lines, axis=0))
        stat_send[0, g, 0] = blocks[2]
        stat_send[1, g, 0] = blocks[0]
        stat_send[0, g, 1] = blocks[1]
        stat_send[1, g, 1] = blocks[1]
        start(near_copy, row_routes, g)
        start(far_copy, far_routes, g)

    def grads(g):
        arrived(near_copy, row_routes, g)
        arrived(far_copy, far_routes, g)
        total = jnp.concatenate(
            [
                stat_send[1, g, 0] + near_recv[0, g, 1] + far_recv[0, g],
                stat_send[0, g, 1] + near_recv[0, g, 0] + near_recv[1, g, 0],
                stat_send[0, g, 0] + near_recv[1, g, 1] + far_recv[1, g],
            ],
            axis=1,
        )
        inverse = 1.0 / total[0:LINES]
        delta = total[LINES:] * inverse
        for i, h in enumerate(range(starts[g], starts[g + 1])):
            q3, do3, kall, _, cols, vcols = operands(h)
            p = e_all[h] * inverse[i : i + 1]
            weight = p.astype(BF16)
            ds = (p * (dp_all[h] - delta[i : i + 1])).astype(BF16)
            ds_all[i] = ds
            dv = plain(weight, do3)
            dk = plain(ds, q3) * scale
            b, lanes = h // hb, slice(h % hb * HD, (h % hb + 1) * HD)
            for kind, (grad, where) in enumerate(((dk, cols), (dv, vcols))):
                for part in range(2):
                    cut = slice(part * (texts // 2), (part + 1) * (texts // 2))
                    text_part[b, part, kind, :, lanes] = grad[cut]
                dkv_send[1, :, where] = grad[texts : texts + columns].astype(BF16)
                dkv_own[:, :, where] = grad[texts + columns : texts + columns + tokens].reshape(frames, columns, HD)
                dkv_send[0, :, where] = grad[texts + columns + tokens :].astype(BF16)
        for b in finished(g):
            core_copy(b).start()
            start_frames(1, b)
        for i, h in enumerate(range(starts[g], starts[g + 1])):
            _, _, kall, _, cols, _ = operands(h)
            dq = both_first(ds_all[i], kall) * scale
            dq_send[1, :, :, cols] = dq[0:tokens].astype(BF16).reshape(frames, columns, HD)
            dq_own[:, :, cols] = dq[tokens : 2 * tokens].reshape(frames, columns, HD)
            dq_send[0, :, :, cols] = dq[2 * tokens :].astype(BF16).reshape(frames, columns, HD)
        start(dq_copy, row_routes, g)

    def core_copy(g):
        return remote(text_part.at[g, 1 - core], core_recv.at[g], core_s.at[g], core_r.at[g], partner)

    def line_of(xx, yy):
        return xx * ny + yy

    def xy_copy(b, xx, yy, source, i):
        where = {"ta": half * nx + xx, "ha": spot(core, yy, z)}
        return remote(xy_own.at[b, line_of(xx, yy)], xy_recv.at[b, source], xy_s.at[b, i], xy_r.at[b, source], where)

    def z_copy(b, target, source, i):
        where = {"ta": (target // RUN) * nx + x, "ha": spot(core, y, lax.rem(target, RUN))}
        return remote(z_own.at[b, target // RUN], z_recv.at[b, source], z_s.at[b, i], z_r.at[b, source], where)

    def all_copy(b, c, yy, source, i):
        where = {"ta": half * nx + b, "ha": spot(c, yy, z)}
        return remote(all_own.at[b], all_recv.at[source], all_s.at[b, i], all_r.at[source], where)

    other_places = [(core, yy) for yy in y_peers] + [(1 - core, lax.rem(y + d, ny)) for d in range(ny)]
    my_line = core * nx * ny + line_of(x, y)

    def text_over_cores(b):
        core_copy(b).wait_recv()
        total = text_part[b, core] + core_recv[b]
        for k in range(nx * ny):
            xy_own[b, k] = total[:, k : k + 1]
        for i, (xx, yy) in enumerate(xy_peers):
            xy_copy(b, xx, yy, line_of(x, y), i).start()

    def text_over_xy(b):
        total = xy_own[b, line_of(x, y)]
        for xx, yy in xy_peers:
            xy_copy(b, x, y, line_of(xx, yy), 0).wait_recv()
        for xx, yy in xy_peers:
            total = total + xy_recv[b, line_of(xx, yy)]
        z_own[b] = total
        for i, target in enumerate(z_peers):
            z_copy(b, target, z_here, i).start()

    def text_over_z(b):
        total = z_own[b, half]
        for source in z_peers:
            z_copy(b, z_here, source, 0).wait_recv()
        for source in z_peers:
            total = total + z_recv[b, source]
        all_own[b] = total
        for i, (c, yy) in enumerate(other_places):
            all_copy(b, c, yy, my_line, i).start()

        @pl.when(b != x)
        def _():
            all_copy(b, core, y, my_line, 2 * ny - 1).start()

        @pl.when(b == x)
        def _():
            all_recv[my_line] = total

    def text_done(b):
        @pl.when(b == x)
        def _():
            for c, xx, yy in near_peers:
                all_copy(b, core, y, c * nx * ny + line_of(xx, yy), 0).wait_recv()
            share = text_out.shape[0]
            spread = all_recv.shape[2]
            where = lax.broadcasted_iota(jnp.int32, (16, spread), 1) - ha * share
            pick = jnp.where(where == lax.broadcasted_iota(jnp.int32, (16, spread), 0), 1.0, 0.0)
            mine = lax.dot_general(
                pick,
                all_recv[...].reshape(-1, spread),
                (((1,), (1,)), ((), ())),
                precision=lax.Precision.HIGHEST,
                preferred_element_type=F32,
            )
            text_out[...] = mine[0:share].astype(BF16)

    def text_sent():
        for b in range(BLOCKS):
            core_copy(b).wait_send()
            for i, (xx, yy) in enumerate(xy_peers):
                xy_copy(b, xx, yy, line_of(x, y), i).wait_send()
            for i, target in enumerate(z_peers):
                z_copy(b, target, z_here, i).wait_send()
            for i, (c, yy) in enumerate(other_places):
                all_copy(b, c, yy, my_line, i).wait_send()

            @pl.when(b != x)
            def _(b=b):
                all_copy(b, core, y, my_line, 2 * ny - 1).wait_send()

    def relay(g):
        @pl.when(g == x)
        def _():
            pass_on(1)

    def fold_rows(c):
        arrived(dq_copy, row_routes, c)
        cols = at(c)
        total = dq_own[:, :, cols] + dq_recv[0, :, :, cols].astype(F32) + dq_recv[1, :, :, cols].astype(F32)
        dq_out[:, 0, :, cols] = total.astype(BF16)

    def fold_frames(b):
        arrived(dkv_copies, frame_routes, b)
        for base in bases:
            where = of(b, base)
            dkv_out[0, 0, :, where] = (dkv_own[0, :, where] + dkv_recv[0, :, where].astype(F32)).astype(BF16)
            dkv_out[1 : frames - 1, 0, :, where] = dkv_own[1 : frames - 1, :, where].astype(BF16)
            dkv_out[frames - 1, 0, :, where] = (
                dkv_own[frames - 1, :, where] + dkv_recv[1, :, where].astype(F32)
            ).astype(BF16)

    count = len(CHUNKS)
    ready = [next(c for c in range(count) if b in finished(c)) + 1 for b in range(BLOCKS)]
    for s in range(count + 6):
        if s < count:
            scores(s)
        if AHEAD <= s + AHEAD < count:
            forward(s + AHEAD)
        if 0 <= s - 1 < count:
            grads(s - 1)
        for lag, stage in (
            (1, text_over_cores),
            (1, relay),
            (2, text_over_xy),
            (3, text_over_z),
            (LAG_FOLD - 1, fold_frames),
            (LAG_FOLD, fold_rows),
            (4, text_done),
        ):
            for b in range(count if stage is fold_rows else BLOCKS):
                if s == lag + (b if stage is fold_rows else ready[b]):
                    stage(b)

    for c in range(count):
        for make, routes in ((row_copies, row_routes), (near_copy, row_routes), (far_copy, far_routes), (dq_copy, row_routes)):
            sent(make, routes, c)
    for b in range(BLOCKS):
        for make in (frame_copies, dkv_copies):
            sent(make, frame_routes, b)
    passed_on(0)
    passed_on(1)
    text_sent()


def attention_grads(nt, nh, query, key_value, out_grad, text_kv, reach, length):
    frames, _, columns, width = query.shape
    tokens = frames * columns
    texts = text_kv.shape[0]
    heads = width // HD
    count = len(CHUNKS)
    bw = width // BLOCKS
    nx, ny = nt // 2, nh // (2 * RUN)
    keys = texts + (frames + 2) * columns
    dma = pltpu.SemaphoreType.DMA
    here = pl.BlockSpec(memory_space=pltpu.VMEM)
    away = pl.BlockSpec(memory_space=pl.ANY)
    return pl.pallas_call(
        functools.partial(attention_kernel, nt, nh),
        out_shape=(
            jax.ShapeDtypeStruct(query.shape, BF16),
            jax.ShapeDtypeStruct(key_value.shape, BF16),
            jax.ShapeDtypeStruct((2 * width // (nt * nh), texts), BF16),
        ),
        in_specs=[away, away, away, here, here, here],
        out_specs=(here, here, here),
        scratch_shapes=[
            pltpu.VMEM((3, frames, columns, width), BF16),
            pltpu.VMEM((3, frames, columns, width), BF16),
            pltpu.VMEM((frames + 2, columns, 2 * width), BF16),
            pltpu.VMEM((keys, 3 * tokens), F32),
            pltpu.VMEM((heads, keys, 3 * tokens), F32),
            pltpu.VMEM((heads, keys, 3 * tokens), F32),
            pltpu.VMEM((max(CHUNKS), keys, 3 * tokens), BF16),
            pltpu.VMEM((2, count, 2, 2 * LINES, tokens), F32),
            pltpu.VMEM((2, count, 2, 2 * LINES, tokens), F32),
            pltpu.VMEM((2, count, 2 * LINES, tokens), F32),
            pltpu.VMEM((2, frames, columns, width), BF16),
            pltpu.VMEM((2, frames, columns, width), BF16),
            pltpu.VMEM((frames, columns, width), F32),
            pltpu.VMEM((2, columns, 2 * width), BF16),
            pltpu.VMEM((2, columns, 2 * width), BF16),
            pltpu.VMEM((frames, columns, 2 * width), F32),
            pltpu.VMEM((2, columns, bw), BF16),
            pltpu.VMEM((2, columns, bw), BF16),
            pltpu.VMEM((BLOCKS, 2, 2, texts // 2, bw), F32),
            pltpu.VMEM((BLOCKS, 2, texts // 2, bw), F32),
            pltpu.VMEM((BLOCKS, nx * ny, 2, 1, bw), F32),
            pltpu.VMEM((BLOCKS, nx * ny, 2, 1, bw), F32),
            pltpu.VMEM((BLOCKS, 2, 1, bw), F32),
            pltpu.VMEM((BLOCKS, 2 * RUN, 1, bw), F32),
            pltpu.VMEM((BLOCKS, 1, bw), F32),
            pltpu.VMEM((texts, 1, bw), F32),
            dma((3,)),
            dma((2, 2, count)),
            dma((2, 2, count)),
            dma((2, 2, BLOCKS)),
            dma((2, 2, BLOCKS)),
            dma((2, count)),
            dma((2, count)),
            dma((2, count)),
            dma((2, count)),
            dma((2, count)),
            dma((2, count)),
            dma((2, 2, BLOCKS)),
            dma((2, 2, BLOCKS)),
            dma((2, 2)),
            dma((2, 2)),
            dma((BLOCKS,)),
            dma((BLOCKS,)),
            dma((BLOCKS, nx * ny)),
            dma((BLOCKS, nx * ny)),
            dma((BLOCKS, 2 * RUN)),
            dma((BLOCKS, 2 * RUN)),
            dma((BLOCKS, 2 * ny)),
            dma((texts,)),
        ],
        compiler_params=pltpu.CompilerParams(collective_id=0, has_side_effects=True, vmem_limit_bytes=LIMIT << 20),
        name="attention_grads",
    )(query, key_value, out_grad, text_kv, reach, length)


def on_device(nt, nh, query, key_value, out_grad, text_kv, tile_reach, text_len):
    query_grad, key_value_grad, text_grad = attention_grads(
        nt, nh, query, key_value, out_grad, text_kv, jnp.transpose(tile_reach, (0, 2, 1)), text_len
    )
    return query_grad, key_value_grad, text_grad.T


def solution(mesh):
    placed = (
        P("ta", "ha", None, None),
        P("ta", "ha", None, None),
        P("ta", "ha", None, None),
        P(),
        P(),
        P(),
    )
    return jax.shard_map(
        functools.partial(on_device, mesh.shape["ta"], mesh.shape["ha"]),
        mesh=mesh,
        in_specs=placed,
        out_specs=(P("ta", "ha", None, None), P("ta", "ha", None, None), P(None, ("ta", "ha"))),
        check_vma=False,
    )
```

```python
import functools
import math

import jax
import jax.numpy as jnp
from jax import lax
from jax.experimental import pallas as pl
from jax.experimental.pallas import tpu as pltpu
from jax.sharding import PartitionSpec as P

HD = 128
MESH = pl.DeviceIdType.MESH
F32 = jnp.float32
BF16 = jnp.bfloat16

CHUNKS = (5, 5, 5, 5)
AHEAD = 3
FIRST = 1
LIMIT = 60
LAG_GRADS = 2
BLOCKS = 4
RUN = 8
LINES = 8


def both_last(a, b):
    return lax.dot_general(a, b, (((1,), (1,)), ((), ())), preferred_element_type=F32)


def both_first(a, b):
    return lax.dot_general(a, b, (((0,), (0,)), ((), ())), preferred_element_type=F32)


def plain(a, b):
    return lax.dot_general(a, b, (((1,), (0,)), ((), ())), preferred_element_type=F32)


def attention_kernel(
    nt,
    nh,
    q_hbm,
    kv_hbm,
    do_hbm,
    text,
    reach,
    length,
    dq_out,
    dkv_out,
    text_out,
    q_all,
    do_all,
    kv_all,
    bias,
    e_all,
    dp_all,
    ds_all,
    stat_send,
    near_recv,
    far_recv,
    dq_send,
    dq_recv,
    dq_own,
    dkv_send,
    dkv_recv,
    dkv_own,
    relay_kv,
    relay_dkv,
    text_part,
    core_recv,
    xy_own,
    xy_recv,
    z_own,
    z_recv,
    all_own,
    all_recv,
    own_sem,
    row_s,
    row_r,
    fr_s,
    fr_r,
    near_s,
    near_r,
    far_s,
    far_r,
    dq_s,
    dq_r,
    dkv_s,
    dkv_r,
    relay_s,
    relay_r,
    core_s,
    core_r,
    xy_s,
    xy_r,
    z_s,
    z_r,
    all_s,
    all_r,
):
    frames, columns = q_all.shape[1], q_all.shape[2]
    width = q_all.shape[3]
    tokens = frames * columns
    texts = text.shape[0]
    heads = width // HD
    starts = [sum(CHUNKS[:c]) for c in range(len(CHUNKS) + 1)]
    hb = heads // BLOCKS
    bw = hb * HD
    scale = 1.0 / math.sqrt(HD)
    keys = texts + (frames + 2) * columns
    ta, ha = lax.axis_index("ta"), lax.axis_index("ha")
    nx = nt // 2
    ny = nh // (2 * RUN)
    half, x = ta // nx, lax.rem(ta, nx)
    core = lax.rem(ha, 2)
    z = lax.rem(ha // 2, RUN)
    y = ha // (2 * RUN)
    first, last = nx - 1, nx
    has_dn, has_up = ha > 0, ha < nh - 1
    has_dn2, has_up2 = ha > 1, ha < nh - 2
    has_prev, has_next = ta > 0, ta < nt - 1
    dn, up = {"ha": ha - 1}, {"ha": ha + 1}
    dn2, up2 = {"ha": ha - 2}, {"ha": ha + 2}
    prev, nxt = {"ta": ta - 1}, {"ta": ta + 1}
    partner = {"ha": ha + 1 - 2 * core}

    def spot(c, yy, zz):
        return (yy * RUN + zz) * 2 + c

    own_copies = [
        pltpu.make_async_copy(q_hbm.at[:, 0], q_all.at[1], own_sem.at[0]),
        pltpu.make_async_copy(do_hbm.at[:, 0], do_all.at[1], own_sem.at[1]),
        pltpu.make_async_copy(kv_hbm.at[:, 0], kv_all.at[pl.ds(1, frames)], own_sem.at[2]),
    ]
    for copy in own_copies:
        copy.start()

    always = ta >= 0
    x_peers = [lax.rem(x + d, nx) for d in range(1, nx)]
    y_peers = [lax.rem(y + d, ny) for d in range(1, ny)]
    xy_peers = [(x, yy) for yy in y_peers] + [(xx, lax.rem(y + d, ny)) for xx in x_peers for d in range(ny)]
    near_peers = [(core, xx, yy) for xx, yy in xy_peers]
    near_peers += [(1 - core, xx, lax.rem(y + d, ny)) for xx in [x] + x_peers for d in range(ny)]
    z_here = half * RUN + z
    z_peers = [lax.rem(z_here + d, 2 * RUN) for d in range(1, 2 * RUN)]
    greet = [(has_dn, dn), (has_up, up), (has_dn2, dn2), (has_up2, up2)]
    greet += [(always, {"ta": half * nx + xx, "ha": spot(c, yy, z)}) for c, xx, yy in near_peers]
    greet += [(always, {"ta": (p // RUN) * nx + x, "ha": spot(core, y, lax.rem(p, RUN))}) for p in z_peers]
    greet += [(ta == first, {"ta": nx + j}) for j in range(nx)]
    greet += [(ta == last, {"ta": j}) for j in range(nx)]
    greet += [(ta < first, {"ta": last}), (ta > last, {"ta": first})]
    barrier = pltpu.get_barrier_semaphore()
    for has, where in greet:

        @pl.when(has)
        def _(where=where):
            pl.semaphore_signal(barrier, inc=1, device_id=where, device_id_type=MESH)

    place = ta * frames
    near_reach = reach[pl.ds(place, frames)].astype(F32)
    near_length = length[pl.ds(pl.multiple_of(place, frames), frames), :].astype(F32)
    token_frame = lax.broadcasted_iota(jnp.int32, (1, tokens), 1) // columns
    row_of = lax.broadcasted_iota(jnp.int32, near_reach.shape, 2)
    pieces = []
    for j, has in ((0, has_dn), (1, always), (2, has_up)):
        found = jnp.sum(jnp.where(row_of == ha + j - 1, near_reach, 0.0), axis=2)
        piece = jnp.full((1, tokens), -1.0, F32)
        for f in range(frames):
            shown = (found[f : f + 1, 1:2] >= abs(j - 1)) & has
            piece = jnp.where((token_frame == f) & shown, found[f : f + 1, 0:1], piece)
        pieces.append(piece)
    limit = jnp.concatenate(pieces, axis=1)
    found = jnp.sum(
        jnp.where(lax.broadcasted_iota(jnp.int32, near_length.shape, 1) == ha, near_length, 0.0), axis=1, keepdims=True
    )
    shown = jnp.zeros((1, tokens), F32)
    for f in range(frames):
        shown = jnp.where(token_frame == f, found[f : f + 1], shown)
    text_limit = jnp.concatenate([jnp.zeros((1, tokens), F32), shown, jnp.zeros((1, tokens), F32)], axis=1)
    line = lax.broadcasted_iota(jnp.int32, (keys, 3 * tokens), 0)
    lane = lax.broadcasted_iota(jnp.int32, (keys, 3 * tokens), 1)
    query_frame = lax.rem(lane, tokens) // columns
    key_frame = (line - texts + columns) // columns - 2
    gap = jnp.abs(key_frame - query_frame).astype(F32)
    inside = ((key_frame >= 0) | has_prev) & ((key_frame < frames) | has_next)
    latent_seen = (line >= texts) & inside & (gap <= limit)
    text_seen = (line < texts) & (line.astype(F32) < text_limit)
    bias[...] = jnp.where(latent_seen | text_seen, 0.0, -1e30)

    pl.semaphore_wait(barrier, sum(has.astype(jnp.int32) for has, _ in greet))

    def at(c):
        return pl.ds(starts[c] * HD, CHUNKS[c] * HD)

    def of(b, base=0):
        return pl.ds(pl.multiple_of(base + b * bw, HD), bw)

    def remote(src, dst, send, recv, where):
        return pltpu.make_async_remote_copy(
            src_ref=src,
            dst_ref=dst,
            send_sem=send,
            recv_sem=recv,
            device_id=where,
            device_id_type=MESH,
        )

    def row_copies(g, side, where):
        slot = 0 if side == 0 else 2
        return [
            remote(
                hbm.at[:, 0, :, at(g)], ref.at[slot, :, :, at(g)], row_s.at[side, i, g], row_r.at[side, i, g], where
            )
            for i, (hbm, ref) in enumerate(((q_hbm, q_all), (do_hbm, do_all)))
        ]

    bases = (0, width)

    def kv_source(g, side, base):
        return kv_hbm.at[frames - 1 if side == 0 else 0, 0, :, of(g, base)]

    def kv_target(g, side, base):
        return kv_all.at[0 if side == 0 else frames + 1, :, of(g, base)]

    def dkv_source(g, side, base):
        return dkv_send.at[side, :, of(g, base)]

    def dkv_target(g, side, base):
        return dkv_recv.at[side, :, of(g, base)]

    def frame_copies(g, side, where):
        return [
            remote(
                kv_source(g, side, base), kv_target(g, side, base), fr_s.at[side, i, g], fr_r.at[side, i, g], where
            )
            for i, base in enumerate(bases)
        ]

    def dkv_copies(g, side, where):
        return [
            remote(
                dkv_source(g, side, base), dkv_target(g, side, base), dkv_s.at[side, i, g], dkv_r.at[side, i, g], where
            )
            for i, base in enumerate(bases)
        ]

    def to_relay(kind, g, side, where):
        source, send, held = ((kv_source, fr_s, relay_kv), (dkv_source, dkv_s, relay_dkv))[kind]
        return [
            remote(source(g, side, base), held.at[i], send.at[side, i, g], relay_r.at[kind, i], where)
            for i, base in enumerate(bases)
        ]

    def from_relay(kind, g, side, where):
        held, target, recv = ((relay_kv, kv_target, fr_r), (relay_dkv, dkv_target, dkv_r))[kind]
        return [
            remote(held.at[i], target(g, side, base), relay_s.at[kind, i], recv.at[side, i, g], where)
            for i, base in enumerate(bases)
        ]

    def near_copy(g, side, where):
        return [remote(stat_send.at[side, g], near_recv.at[side, g], near_s.at[side, g], near_r.at[side, g], where)]

    def far_copy(g, side, where):
        return [remote(stat_send.at[side, g, 0], far_recv.at[side, g], far_s.at[side, g], far_r.at[side, g], where)]

    def dq_copy(g, side, where):
        return [
            remote(
                dq_send.at[side, :, :, at(g)], dq_recv.at[side, :, :, at(g)], dq_s.at[side, g], dq_r.at[side, g], where
            )
        ]

    row_routes = ((0, has_up, up, has_dn), (1, has_dn, dn, has_up))
    far_routes = ((0, has_up2, up2, has_dn2), (1, has_dn2, dn2, has_up2))
    frame_routes = ((0, has_next, nxt, has_prev), (1, has_prev, prev, has_next))
    crossings = ((0, ta == first, nxt), (1, ta == last, prev))

    def start(make, routes, g):
        for side, has, where, _ in routes:

            @pl.when(has)
            def _(side=side, where=where):
                for copy in make(g, side, where):
                    copy.start()

    def arrived(make, routes, g):
        for side, _, where, has in routes:

            @pl.when(has)
            def _(side=side, where=where):
                for copy in make(g, side, where):
                    copy.wait_recv()

    def sent(make, routes, g):
        for side, has, where, _ in routes:

            @pl.when(has)
            def _(side=side, where=where):
                for copy in make(g, side, where):
                    copy.wait_send()

    def start_frames(kind, g):
        make = (frame_copies, dkv_copies)[kind]
        for (side, has, where, _), (_, crosses, _) in zip(frame_routes, crossings):
            relayed = crosses & (g != x)

            @pl.when(has & jnp.logical_not(relayed))
            def _(side=side, where=where):
                for copy in make(g, side, where):
                    copy.start()

            @pl.when(relayed)
            def _(side=side):
                for copy in to_relay(kind, g, side, {"ta": half * nx + g}):
                    copy.start()

    relays = ((0, (half == 0) & (ta != first), {"ta": last}), (1, (half == 1) & (ta != last), {"ta": first}))

    def pass_on(kind):
        for side, has, where in relays:

            @pl.when(has)
            def _(side=side, where=where):
                for copy in to_relay(kind, x, side, where):
                    copy.wait_recv()
                for copy in from_relay(kind, x, side, where):
                    copy.start()

    def passed_on(kind):
        for side, has, where in relays:

            @pl.when(has)
            def _(side=side, where=where):
                for copy in from_relay(kind, x, side, where):
                    copy.wait_send()

    def forward(g):
        start(row_copies, row_routes, g)

    for b in range(BLOCKS):
        start_frames(0, b)
    for g in range(FIRST):
        forward(g)

    for side, _, _, has in row_routes:

        @pl.when(jnp.logical_not(has))
        def _(side=side):
            slot = 0 if side == 0 else 2
            q_all[slot] = jnp.zeros(q_all.shape[1:], BF16)
            do_all[slot] = jnp.zeros(do_all.shape[1:], BF16)
            near_recv[side, :, 0] = jnp.zeros((len(CHUNKS),) + near_recv.shape[3:], F32)
            near_recv[side, :, 1] = jnp.ones((len(CHUNKS),) + near_recv.shape[3:], F32)
            dq_recv[side] = jnp.zeros(dq_recv.shape[1:], BF16)

    for side, _, _, has in far_routes:

        @pl.when(jnp.logical_not(has))
        def _(side=side):
            far_recv[side] = jnp.zeros(far_recv.shape[1:], F32)

    for side, _, _, has in frame_routes:

        @pl.when(jnp.logical_not(has))
        def _(side=side):
            slot = 0 if side == 0 else frames + 1
            kv_all[slot] = jnp.zeros(kv_all.shape[1:], BF16)
            dkv_recv[side] = jnp.zeros(dkv_recv.shape[1:], BF16)

    pass_on(0)
    for g in range(FIRST, AHEAD):
        forward(g)
    for copy in own_copies:
        copy.wait()

    def operands(h):
        cols, vcols = pl.ds(h * HD, HD), pl.ds(width + h * HD, HD)
        q3 = q_all[:, :, :, cols].reshape(3 * tokens, HD)
        do3 = do_all[:, :, :, cols].reshape(3 * tokens, HD)
        kall = jnp.concatenate([text[:, cols], kv_all[:, :, cols].reshape(-1, HD)], axis=0)
        vall = jnp.concatenate([text[:, vcols], kv_all[:, :, vcols].reshape(-1, HD)], axis=0)
        return q3, do3, kall, vall, cols, vcols

    def finished(g):
        return [b for b in range(BLOCKS) if starts[g] < (b + 1) * hb <= starts[g + 1]]

    def scores(g):
        for b in range(BLOCKS):
            if starts[g] <= b * hb < starts[g + 1]:
                arrived(frame_copies, frame_routes, b)
        arrived(row_copies, row_routes, g)
        sums = []
        hg = CHUNKS[g]
        for h in range(starts[g], starts[g + 1]):
            q3, do3, kall, vall, _, _ = operands(h)
            s = both_last(kall, q3)
            dp = both_last(vall, do3)
            e = jnp.exp(s * scale + bias[...])
            e_all[h] = e
            dp_all[h] = dp
            sums.append((jnp.sum(e, axis=0, keepdims=True), jnp.sum(e * dp, axis=0, keepdims=True)))
        filler = [jnp.ones((1, tokens), F32)] * (LINES - hg)
        blocks = []
        for part in range(3):
            cut = slice(part * tokens, (part + 1) * tokens)
            lines = [a[:, cut] for a, _ in sums] + filler + [b[:, cut] for _, b in sums] + filler
            blocks.append(jnp.concatenate(lines, axis=0))
        stat_send[0, g, 0] = blocks[2]
        stat_send[1, g, 0] = blocks[0]
        stat_send[0, g, 1] = blocks[1]
        stat_send[1, g, 1] = blocks[1]
        start(near_copy, row_routes, g)
        start(far_copy, far_routes, g)

    def grads(g):
        arrived(near_copy, row_routes, g)
        arrived(far_copy, far_routes, g)
        total = jnp.concatenate(
            [
                stat_send[1, g, 0] + near_recv[0, g, 1] + far_recv[0, g],
                stat_send[0, g, 1] + near_recv[0, g, 0] + near_recv[1, g, 0],
                stat_send[0, g, 0] + near_recv[1, g, 1] + far_recv[1, g],
            ],
            axis=1,
        )
        inverse = 1.0 / total[0:LINES]
        delta = total[LINES:] * inverse
        for i, h in enumerate(range(starts[g], starts[g + 1])):
            q3, do3, kall, _, cols, vcols = operands(h)
            p = e_all[h] * inverse[i : i + 1]
            weight = p.astype(BF16)
            ds = (p * (dp_all[h] - delta[i : i + 1])).astype(BF16)
            ds_all[i] = ds
            dv = plain(weight, do3)
            dk = plain(ds, q3) * scale
            b, lanes = h // hb, slice(h % hb * HD, (h % hb + 1) * HD)
            for kind, (grad, where) in enumerate(((dk, cols), (dv, vcols))):
                for part in range(2):
                    cut = slice(part * (texts // 2), (part + 1) * (texts // 2))
                    text_part[b, part, kind, :, lanes] = grad[cut]
                dkv_send[1, :, where] = grad[texts : texts + columns].astype(BF16)
                dkv_own[:, :, where] = grad[texts + columns : texts + columns + tokens].reshape(frames, columns, HD)
                dkv_send[0, :, where] = grad[texts + columns + tokens :].astype(BF16)
        for b in finished(g):
            core_copy(b).start()
            start_frames(1, b)
        for i, h in enumerate(range(starts[g], starts[g + 1])):
            _, _, kall, _, cols, _ = operands(h)
            dq = both_first(ds_all[i], kall) * scale
            dq_send[1, :, :, cols] = dq[0:tokens].astype(BF16).reshape(frames, columns, HD)
            dq_own[:, :, cols] = dq[tokens : 2 * tokens].reshape(frames, columns, HD)
            dq_send[0, :, :, cols] = dq[2 * tokens :].astype(BF16).reshape(frames, columns, HD)
        start(dq_copy, row_routes, g)

    def core_copy(g):
        return remote(text_part.at[g, 1 - core], core_recv.at[g], core_s.at[g], core_r.at[g], partner)

    def line_of(xx, yy):
        return xx * ny + yy

    def xy_copy(b, xx, yy, source, i):
        where = {"ta": half * nx + xx, "ha": spot(core, yy, z)}
        return remote(xy_own.at[b, line_of(xx, yy)], xy_recv.at[b, source], xy_s.at[b, i], xy_r.at[b, source], where)

    def z_copy(b, target, source, i):
        where = {"ta": (target // RUN) * nx + x, "ha": spot(core, y, lax.rem(target, RUN))}
        return remote(z_own.at[b, target // RUN], z_recv.at[b, source], z_s.at[b, i], z_r.at[b, source], where)

    def all_copy(b, c, yy, source, i):
        where = {"ta": half * nx + b, "ha": spot(c, yy, z)}
        return remote(all_own.at[b], all_recv.at[source], all_s.at[b, i], all_r.at[source], where)

    other_places = [(core, yy) for yy in y_peers] + [(1 - core, lax.rem(y + d, ny)) for d in range(ny)]
    my_line = core * nx * ny + line_of(x, y)

    def text_over_cores(b):
        core_copy(b).wait_recv()
        total = text_part[b, core] + core_recv[b]
        for k in range(nx * ny):
            xy_own[b, k] = total[:, k : k + 1]
        for i, (xx, yy) in enumerate(xy_peers):
            xy_copy(b, xx, yy, line_of(x, y), i).start()

    def text_over_xy(b):
        total = xy_own[b, line_of(x, y)]
        for xx, yy in xy_peers:
            xy_copy(b, x, y, line_of(xx, yy), 0).wait_recv()
        for xx, yy in xy_peers:
            total = total + xy_recv[b, line_of(xx, yy)]
        z_own[b] = total
        for i, target in enumerate(z_peers):
            z_copy(b, target, z_here, i).start()

    def text_over_z(b):
        total = z_own[b, half]
        for source in z_peers:
            z_copy(b, z_here, source, 0).wait_recv()
        for source in z_peers:
            total = total + z_recv[b, source]
        all_own[b] = total
        for i, (c, yy) in enumerate(other_places):
            all_copy(b, c, yy, my_line, i).start()

        @pl.when(b != x)
        def _():
            all_copy(b, core, y, my_line, 2 * ny - 1).start()

        @pl.when(b == x)
        def _():
            all_recv[my_line] = total

    def text_done(b):
        @pl.when(b == x)
        def _():
            for c, xx, yy in near_peers:
                all_copy(b, core, y, c * nx * ny + line_of(xx, yy), 0).wait_recv()
            share = text_out.shape[0]
            spread = all_recv.shape[2]
            where = lax.broadcasted_iota(jnp.int32, (16, spread), 1) - ha * share
            pick = jnp.where(where == lax.broadcasted_iota(jnp.int32, (16, spread), 0), 1.0, 0.0)
            mine = lax.dot_general(
                pick,
                all_recv[...].reshape(-1, spread),
                (((1,), (1,)), ((), ())),
                precision=lax.Precision.HIGHEST,
                preferred_element_type=F32,
            )
            text_out[...] = mine[0:share].astype(BF16)

    def text_sent():
        for b in range(BLOCKS):
            core_copy(b).wait_send()
            for i, (xx, yy) in enumerate(xy_peers):
                xy_copy(b, xx, yy, line_of(x, y), i).wait_send()
            for i, target in enumerate(z_peers):
                z_copy(b, target, z_here, i).wait_send()
            for i, (c, yy) in enumerate(other_places):
                all_copy(b, c, yy, my_line, i).wait_send()

            @pl.when(b != x)
            def _(b=b):
                all_copy(b, core, y, my_line, 2 * ny - 1).wait_send()

    def relay(g):
        @pl.when(g == x)
        def _():
            pass_on(1)

    def fold_rows(c):
        arrived(dq_copy, row_routes, c)
        cols = at(c)
        total = dq_own[:, :, cols] + dq_recv[0, :, :, cols].astype(F32) + dq_recv[1, :, :, cols].astype(F32)
        dq_out[:, 0, :, cols] = total.astype(BF16)

    def fold_frames(b):
        arrived(dkv_copies, frame_routes, b)
        for base in bases:
            where = of(b, base)
            dkv_out[0, 0, :, where] = (dkv_own[0, :, where] + dkv_recv[0, :, where].astype(F32)).astype(BF16)
            dkv_out[1 : frames - 1, 0, :, where] = dkv_own[1 : frames - 1, :, where].astype(BF16)
            dkv_out[frames - 1, 0, :, where] = (
                dkv_own[frames - 1, :, where] + dkv_recv[1, :, where].astype(F32)
            ).astype(BF16)

    count = len(CHUNKS)
    ready = [next(c for c in range(count) if b in finished(c)) + LAG_GRADS for b in range(BLOCKS)]
    for s in range(count + LAG_GRADS + 5):
        if s < count:
            scores(s)
        if AHEAD <= s + AHEAD < count:
            forward(s + AHEAD)
        if 0 <= s - LAG_GRADS < count:
            grads(s - LAG_GRADS)
        for lag, stage in (
            (1, text_over_cores),
            (1, relay),
            (2, text_over_xy),
            (3, text_over_z),
            (3, fold_frames),
            (LAG_GRADS + 3, fold_rows),
            (4, text_done),
        ):
            for b in range(count if stage is fold_rows else BLOCKS):
                if s == lag + (b if stage is fold_rows else ready[b]):
                    stage(b)

    for c in range(count):
        for make, routes in ((row_copies, row_routes), (near_copy, row_routes), (far_copy, far_routes), (dq_copy, row_routes)):
            sent(make, routes, c)
    for b in range(BLOCKS):
        for make in (frame_copies, dkv_copies):
            sent(make, frame_routes, b)
    passed_on(0)
    passed_on(1)
    text_sent()


def attention_grads(nt, nh, query, key_value, out_grad, text_kv, reach, length):
    frames, _, columns, width = query.shape
    tokens = frames * columns
    texts = text_kv.shape[0]
    heads = width // HD
    count = len(CHUNKS)
    bw = width // BLOCKS
    nx, ny = nt // 2, nh // (2 * RUN)
    keys = texts + (frames + 2) * columns
    dma = pltpu.SemaphoreType.DMA
    here = pl.BlockSpec(memory_space=pltpu.VMEM)
    away = pl.BlockSpec(memory_space=pl.ANY)
    return pl.pallas_call(
        functools.partial(attention_kernel, nt, nh),
        out_shape=(
            jax.ShapeDtypeStruct(query.shape, BF16),
            jax.ShapeDtypeStruct(key_value.shape, BF16),
            jax.ShapeDtypeStruct((2 * width // (nt * nh), texts), BF16),
        ),
        in_specs=[away, away, away, here, here, here],
        out_specs=(here, here, here),
        scratch_shapes=[
            pltpu.VMEM((3, frames, columns, width), BF16),
            pltpu.VMEM((3, frames, columns, width), BF16),
            pltpu.VMEM((frames + 2, columns, 2 * width), BF16),
            pltpu.VMEM((keys, 3 * tokens), F32),
            pltpu.VMEM((heads, keys, 3 * tokens), F32),
            pltpu.VMEM((heads, keys, 3 * tokens), F32),
            pltpu.VMEM((max(CHUNKS), keys, 3 * tokens), BF16),
            pltpu.VMEM((2, count, 2, 2 * LINES, tokens), F32),
            pltpu.VMEM((2, count, 2, 2 * LINES, tokens), F32),
            pltpu.VMEM((2, count, 2 * LINES, tokens), F32),
            pltpu.VMEM((2, frames, columns, width), BF16),
            pltpu.VMEM((2, frames, columns, width), BF16),
            pltpu.VMEM((frames, columns, width), F32),
            pltpu.VMEM((2, columns, 2 * width), BF16),
            pltpu.VMEM((2, columns, 2 * width), BF16),
            pltpu.VMEM((frames, columns, 2 * width), F32),
            pltpu.VMEM((2, columns, bw), BF16),
            pltpu.VMEM((2, columns, bw), BF16),
            pltpu.VMEM((BLOCKS, 2, 2, texts // 2, bw), F32),
            pltpu.VMEM((BLOCKS, 2, texts // 2, bw), F32),
            pltpu.VMEM((BLOCKS, nx * ny, 2, 1, bw), F32),
            pltpu.VMEM((BLOCKS, nx * ny, 2, 1, bw), F32),
            pltpu.VMEM((BLOCKS, 2, 1, bw), F32),
            pltpu.VMEM((BLOCKS, 2 * RUN, 1, bw), F32),
            pltpu.VMEM((BLOCKS, 1, bw), F32),
            pltpu.VMEM((texts, 1, bw), F32),
            dma((3,)),
            dma((2, 2, count)),
            dma((2, 2, count)),
            dma((2, 2, BLOCKS)),
            dma((2, 2, BLOCKS)),
            dma((2, count)),
            dma((2, count)),
            dma((2, count)),
            dma((2, count)),
            dma((2, count)),
            dma((2, count)),
            dma((2, 2, BLOCKS)),
            dma((2, 2, BLOCKS)),
            dma((2, 2)),
            dma((2, 2)),
            dma((BLOCKS,)),
            dma((BLOCKS,)),
            dma((BLOCKS, nx * ny)),
            dma((BLOCKS, nx * ny)),
            dma((BLOCKS, 2 * RUN)),
            dma((BLOCKS, 2 * RUN)),
            dma((BLOCKS, 2 * ny)),
            dma((texts,)),
        ],
        compiler_params=pltpu.CompilerParams(collective_id=0, has_side_effects=True, vmem_limit_bytes=LIMIT << 20),
        name="attention_grads",
    )(query, key_value, out_grad, text_kv, reach, length)


def on_device(nt, nh, query, key_value, out_grad, text_kv, tile_reach, text_len):
    query_grad, key_value_grad, text_grad = attention_grads(
        nt, nh, query, key_value, out_grad, text_kv, jnp.transpose(tile_reach, (0, 2, 1)), text_len
    )
    return query_grad, key_value_grad, text_grad.T


def solution(mesh):
    placed = (
        P("ta", "ha", None, None),
        P("ta", "ha", None, None),
        P("ta", "ha", None, None),
        P(),
        P(),
        P(),
    )
    return jax.shard_map(
        functools.partial(on_device, mesh.shape["ta"], mesh.shape["ha"]),
        mesh=mesh,
        in_specs=placed,
        out_specs=(P("ta", "ha", None, None), P("ta", "ha", None, None), P(None, ("ta", "ha"))),
        check_vma=False,
    )
```
